512 devices in a mesh: member: 8 (over y_hi, x), lat: 64 (over y_lo, z, core).
Axes of the slice: x: 4, y: 8 (y_hi: 2, y_lo: 4; y = y_hi * 4 + y_lo), z: 8, core: 2. Of those that a mesh axis runs over, the one named last changes fastest.
Arguments:
- atmosphere: float32 [2, 16, 8, 384, 1536], P(None, 'member', None, 'lat'), may hold values from -4 to 4
- ocean_state: float32 [2, 384, 1536], P(None, 'lat', 'member'), may hold values from -4 to 4
- viscosity: float32 [384, 1536], P('lat', 'member'), may hold values from 0.02 to 0.2
- sea_mask: int32 [384, 1536], P('lat'), may hold values 0 or 1
- parameter_index: int32 [16], P('member'), may hold values from 0 to 31
- parameter_table: float32 [32, 3], replicated, may hold values from 0.1 to 0.3
- level_mix: float32 [8, 8], replicated, may hold values from -0.5 to 0.5
Outputs:
- atmos_out: float32 [2, 16, 8, 384, 1536], P(None, 'member', None, 'lat')
- ocean_out: float32 [2, 384, 1536], P(None, 'lat', 'member')
The draws below stay inside these ranges and needn't reach their ends.
All inputs are finite; a program needn't handle non-finite values. No bound on the sum of `sea_mask` on one device may be relied on, other than what follows from the above.
Results may differ from the reference program's by a relative error of at most 0.00011.
Values sent between devices are 32-bit elements; how exact they have to be, the bound alone decides.
A program may use at most 64 MiB of HBM per device.

```python
import math
import jax
import jax.numpy as jnp
from jax import lax

LEV = 8
LON = 1536
SETS = 32
PCOUNT = 3
ASTEPS = 3
OSTEPS = 2
COUPLE = 2
MEMBERS = 16
NLAT = 384


def touch_ends(drawn, stream_key, low, high):
    spot = [jax.random.randint(jax.random.fold_in(stream_key, axis), (), 0, length) for axis, length in enumerate(drawn.shape)]
    longest = drawn.shape.index(max(drawn.shape))
    beside = spot[:longest] + [(spot[longest] + 1) % drawn.shape[longest]] + spot[longest + 1:]
    return drawn.at[tuple(spot)].set(low).at[tuple(beside)].set(high)


def block_levels(key, extent, split, least, largest):
    loudness = 1.0
    for position, parts in split:
        heights = jax.random.uniform(jax.random.fold_in(jax.random.fold_in(key, 6), position), (parts,), jnp.float32, least / len(split), largest / len(split))
        loudness = loudness * jnp.repeat(jnp.exp(heights), extent[position] // parts).reshape((-1,) + (1,) * (len(extent) - 1 - position))
    return loudness


def bell_draw(own_key, extent, deviation, bound, cuts=(), kind=jnp.bfloat16):
    drawn = jax.random.normal(own_key, extent, jnp.float32) * deviation
    if len(cuts) > 0:
        drawn = block_levels(own_key, extent, cuts, -0.22, 0.18) * drawn
    return jnp.clip(drawn, min=-bound, max=bound).astype(kind)


def setup_inputs(seed: int = 0) -> dict:
    key_of = jax.random.split(jax.random.key(seed), 8)
    return {
        "atmosphere": bell_draw(key_of[0], (2, MEMBERS, LEV, NLAT, LON), 1.0, 4.0, ((1, 8), (3, 64)), jnp.float32),
        "ocean_state": bell_draw(key_of[1], (2, NLAT, LON), 1.0, 4.0, ((1, 64), (2, 8)), jnp.float32),
        "viscosity": jnp.clip(jnp.exp(math.log(0.2) - 2.3025851 * jax.random.uniform(key_of[2], (NLAT, LON), jnp.float32) ** block_levels(key_of[2], (NLAT, LON), ((0, 64), (1, 8)), -0.2, 0.2)), 0.02, 0.2),
        "sea_mask": touch_ends((jax.random.randint(key_of[3], (NLAT, LON), 0, 3) < 2).astype(jnp.int32), jax.random.fold_in(key_of[3], 1), 0, 1),
        "parameter_index": touch_ends(jax.random.randint(key_of[4], (MEMBERS,), 0, SETS), jax.random.fold_in(key_of[4], 1), 0, SETS - 1).astype(jnp.int32),
        "parameter_table": jnp.clip(jnp.exp(jax.random.uniform(key_of[5], (SETS, PCOUNT), jnp.float32, math.log(0.1), math.log(0.3))), 0.1, 0.3),
        "level_mix": bell_draw(key_of[6], (LEV, LEV), 0.1, 0.5, (), jnp.float32),
    }


ADVECTION = 0.1
OCEAN_GAIN = 0.5
OCEAN_DIFFUSION = 0.15


def lookup(parameter_index, parameter_table):
    onehot = (parameter_index[:, None] == jnp.arange(parameter_table.shape[0], dtype=jnp.int32)[None, :]).astype(jnp.float32)
    picked = jnp.dot(onehot, parameter_table, precision=lax.Precision.HIGHEST, preferred_element_type=jnp.float32)
    return 0.6 * picked[:, 0], 2.0 * jnp.transpose(picked[:, 1:3])


def atmos_step(padded_rows, surface, diffusivity, exchange, level_mix):
    centre = padded_rows[:, :, :, 1:-1, :]
    northern = padded_rows[:, :, :, 2:, :]
    southern = padded_rows[:, :, :, :-2, :]
    eastern = jnp.roll(centre, -1, axis=4)
    western = jnp.roll(centre, 1, axis=4)
    laplace = eastern + western + northern + southern - 4.0 * centre
    zonal_wind = centre[1]
    advected = centre - ADVECTION * zonal_wind[None] * (eastern - western) * 0.5 + diffusivity[None, :, None, None, None] * laplace
    mixed_state = advected + jnp.einsum("kl,fmlrn->fmkrn", level_mix, advected, precision=lax.Precision.HIGHEST)
    bottom = mixed_state[:, :, 0] + exchange[:, :, None, None] * (surface[:, None] - mixed_state[:, :, 0])
    return mixed_state.at[:, :, 0].set(bottom)


def reference(atmosphere, ocean_state, viscosity, sea_mask, parameter_index, parameter_table, level_mix):
    diffusivity, exchange = lookup(parameter_index, parameter_table)
    ocean_mask = sea_mask.astype(jnp.float32)
    ocean_rate = jnp.stack([jnp.full_like(viscosity, OCEAN_DIFFUSION), viscosity])
    atmos_state = atmosphere
    ocean = ocean_state
    for coupling in range(COUPLE):
        surface = ocean
        for substep in range(ASTEPS):
            padded_rows = jnp.pad(atmos_state, ((0, 0), (0, 0), (0, 0), (1, 1), (0, 0)))
            atmos_state = atmos_step(padded_rows, surface, diffusivity, exchange, level_mix)
        flux_terms = jnp.sum(exchange[:, :, None, None] * (atmos_state[:, :, 0] - surface[:, None]), axis=1)
        forcing = flux_terms / MEMBERS
        for substep in range(OSTEPS):
            padded_ocean = jnp.pad(ocean, ((0, 0), (1, 1), (0, 0)))
            laplace = padded_ocean[:, 2:] + padded_ocean[:, :-2] + jnp.roll(ocean, -1, axis=2) + jnp.roll(ocean, 1, axis=2) - 4.0 * ocean
            ocean = ocean + ocean_mask[None] * (OCEAN_GAIN * forcing + ocean_rate * laplace)
    return atmos_state, ocean
```

```python
import functools

import jax
import jax.numpy as jnp
from jax import lax
from jax.experimental import pallas as pl
from jax.experimental.pallas import tpu as pltpu
from jax.sharding import PartitionSpec as P

ADVECTION = 0.1
OCEAN_GAIN = 0.5
OCEAN_DIFFUSION = 0.15
MESH = pl.DeviceIdType.MESH
F32 = jnp.float32
LANES = 128
CHUNK = 512


def tiles(vector, count):
    return jnp.concatenate([vector] * count, axis=1)


def sublane(shape):
    return lax.broadcasted_iota(jnp.int32, shape, 0)


def stack_rows(south, own, north):
    index = sublane(own.shape)
    middle = pltpu.roll(own, 4, 0)
    low = jnp.where(index < 4, pltpu.roll(south, 6, 0), middle)
    high = jnp.where(index < 2, middle, pltpu.roll(north, 2, 0))
    return jnp.concatenate([low, high], axis=0)


def join_chunks(even, odd):
    lane = lax.broadcasted_iota(jnp.int32, (8, LANES), 1)
    first = pltpu.roll(odd[:, :LANES], 64, 1)
    second = pltpu.roll(odd[:, LANES:], 64, 1)
    return jnp.concatenate(
        [even[:, :LANES], jnp.where(lane < 64, even[:, LANES:], first), jnp.where(lane < 64, first, second)], axis=1
    )


def kernel(
    nx, nlat, scale,
    atm, ocean_in, visc_in, mask_in, pick, table, mixing, atm_out, ocean_out,
    state, coef, diff, surf, chunks, masks, ocean, visc, mask, force, part, gather_x, total, gather_y, gather_f, seg,
    load_sem, halo_send, halo_recv, seg_send, seg_recv, pair_send, pair_recv, mask_send, mask_recv,
    x_send, x_recv, y_send, y_recv, f_send, f_recv, out_sem,
):
    me = lax.axis_index("member")
    lat = lax.axis_index("lat")
    x, yh = lax.rem(me, nx), lax.div(me, nx)
    has_south, has_north = lat > 0, lat < nlat - 1
    partner = ((1 - yh) * nx + x, lat)
    lon = mask_in.shape[1]
    pieces = lon // CHUNK
    quarter = lon // nx

    def peers():
        for side in (-1, 0, 1):
            for step in range(nx):
                if side or step:
                    yield side, step, (yh * nx + lax.rem(x + step, nx), lat + side)

    def guarded(side, run):
        if side < 0:
            pl.when(has_south)(run)
        elif side > 0:
            pl.when(has_north)(run)
        else:
            run()

    loads = [pltpu.make_async_copy(atm.at[:, :, r], state.at[0, r + 3], load_sem.at[r]) for r in range(6)]
    for load in loads:
        load.start()

    barrier = pltpu.get_barrier_semaphore()
    pl.semaphore_signal(barrier, inc=1, device_id=partner, device_id_type=MESH)
    for side, step, device in peers():
        guarded(side, lambda device=device: pl.semaphore_signal(barrier, inc=1, device_id=device, device_id_type=MESH))

    lane_pad = jnp.zeros((8, 2 * LANES), F32)
    for field in range(3):
        seg[field] = lane_pad
        for r in range(6):
            line = visc_in[r : r + 1, :] if field == 2 else ocean_in[r, field : field + 1, :]
            seg[field, r : r + 1, 0:192] = line
    masks[1] = jnp.zeros((8, lon), F32)
    masks[1, 0:6, :] = mask_in[...].astype(F32)
    row_zero = jnp.zeros((2, 2, 8, lon), F32)

    @pl.when(lat == 0)
    def _():
        for b in range(6):
            state[b, 2] = row_zero
        masks[0] = jnp.zeros((8, lon), F32)
        for a in range(2):
            for i in range(nx):
                chunks[a, 0, i] = jnp.zeros((3, 8, 2 * LANES), F32)
                gather_f[a, 0, i] = jnp.zeros((2, 8, quarter), F32)

    @pl.when(lat == nlat - 1)
    def _():
        for b in range(6):
            state[b, 9] = row_zero
        masks[2] = jnp.zeros((8, lon), F32)
        for a in range(2):
            for i in range(nx):
                chunks[a, 2, i] = jnp.zeros((3, 8, 2 * LANES), F32)
                gather_f[a, 2, i] = jnp.zeros((2, 8, quarter), F32)

    pl.semaphore_wait(barrier, nx + nx * has_south.astype(jnp.int32) + nx * has_north.astype(jnp.int32))

    def halo(cp, side, depth):
        row = 5 - depth if side > 0 else depth
        there = 2 - depth if side > 0 else 9 + depth
        source = atm.at[:, :, row] if cp == 0 else state.at[3, row + 3]
        k = (side + 1) // 2
        return pltpu.make_async_remote_copy(
            source, state.at[3 * cp, there], halo_send.at[cp, k, depth], halo_recv.at[cp, k, depth],
            device_id=(me, lat + side), device_id_type=MESH,
        )

    def start_halos(cp):
        for depth in range(3):
            for side in (-1, 1):
                guarded(side, lambda side=side, depth=depth: halo(cp, side, depth).start())

    def wait_halo(cp, depth):
        for side in (-1, 1):
            guarded(-side, lambda side=side: halo(cp, side, depth).wait_recv())

    def spread(stage, side, step, device):
        source = seg if stage == 0 else chunks.at[1 - yh, 1, x]
        target = chunks.at[yh if stage == 0 else 1 - yh, 1 - side, x]
        return pltpu.make_async_remote_copy(
            source, target, seg_send.at[stage, side + 1, step], seg_recv.at[stage, side + 1, step],
            device_id=device, device_id_type=MESH,
        )

    pair = pltpu.make_async_remote_copy(
        seg, chunks.at[yh, 1, x], pair_send, pair_recv, device_id=partner, device_id_type=MESH
    )

    def send_mask(side):
        return pltpu.make_async_remote_copy(
            masks.at[1], masks.at[1 - side], mask_send.at[(side + 1) // 2], mask_recv.at[(side + 1) // 2],
            device_id=(me, lat + side), device_id_type=MESH,
        )

    pair.start()
    start_halos(0)
    for side, step, device in peers():
        guarded(side, lambda a=(side, step, device): spread(0, *a).start())
    for side in (-1, 1):
        guarded(side, lambda side=side: send_mask(side).start())
    chunks[yh, 1, x] = seg[...]

    sub = sublane((8, LANES))
    top = sub == 0
    dif = [0.6 * table[0, pick[m]] for m in range(2)]
    exc = [[2.0 * table[1 + c, pick[m]] for m in range(2)] for c in range(2)]
    exv = [[jnp.where(top, exc[c][m], 0.0) for m in range(2)] for c in range(2)]
    mix = mixing[...]
    row8 = lax.broadcasted_iota(jnp.int32, (8, 8), 0)
    col8 = lax.broadcasted_iota(jnp.int32, (8, 8), 1)
    for m in range(2):
        diff[m, 0] = jnp.full((8, LANES), dif[m], F32)
        diff[m, 1] = jnp.full((8, LANES), 1.0 - 4.0 * dif[m], F32)
    for r in range(8):
        diagonal = jnp.sum(jnp.where(col8 == lax.rem(row8 - r + 8, 8), mix, 0.0), axis=1, keepdims=True)
        value = jnp.broadcast_to(diagonal, (8, LANES))
        if r == 0:
            value = value + 1.0
        for c in range(2):
            for m in range(2):
                coef[c, m, r] = jnp.where(top, value * (1.0 - exc[c][m]), value)

    def unit(source, target, row, m, k, with_surface):
        e = row + 3
        width = CHUNK // LANES
        off = pl.multiple_of(k * CHUNK, CHUNK)
        right = pl.multiple_of(lax.rem(k + 1, pieces) * CHUNK, LANES)
        left = pl.multiple_of(lax.rem(k * CHUNK + lon - LANES, lon), LANES)
        d = tiles(diff[m, 0], width)
        d4 = tiles(diff[m, 1], width)
        wind = None
        for c in (1, 0):
            centre = state[source, e, c, m, :, pl.ds(off, CHUNK)]
            ahead = state[source, e, c, m, :, pl.ds(right, LANES)]
            behind = state[source, e, c, m, :, pl.ds(left, LANES)]
            north = state[source, e + 1, c, m, :, pl.ds(off, CHUNK)]
            south = state[source, e - 1, c, m, :, pl.ds(off, CHUNK)]
            east = pltpu.roll(jnp.concatenate([centre, ahead], axis=1), CHUNK + LANES - 1, 1)[:, :CHUNK]
            west = pltpu.roll(jnp.concatenate([centre, behind], axis=1), 1, 1)[:, :CHUNK]
            if c == 1:
                wind = (ADVECTION * 0.5) * centre
            advected = d4 * centre + d * ((east + west) + (north + south)) - wind * (east - west)
            value = tiles(coef[c, m, 0], width) * advected
            for r in range(1, 8):
                value = value + tiles(coef[c, m, r], width) * pltpu.roll(advected, r, 0)
            if with_surface:
                value = value + surf[row + 2, c, m, :, pl.ds(off, CHUNK)]
            state[target, e, c, m, :, pl.ds(off, CHUNK)] = value

    def rows(source, target, first, stride, count, with_surface):
        each = 2 * pieces

        def body(t, carry):
            row = first + (t // each) * stride
            m = lax.rem(t // pieces, 2)
            k = lax.rem(t, pieces)
            inside = ((row >= 0) | has_south) & ((row <= 5) | has_north)

            @pl.when(inside)
            def _():
                unit(source, target, row, m, k, with_surface)

            return carry

        lax.fori_loop(0, count * each, body, 0)

    def add_surface(target):
        for row in range(-2, 8):
            for c in range(2):
                line = jnp.broadcast_to(ocean[c, row + 4 : row + 5, :], (8, lon))
                for m in range(2):
                    value = tiles(exv[c][m], lon // LANES) * line
                    surf[row + 2, c, m] = value

                    def run(value=value, c=c, m=m, row=row):
                        state[target, row + 3, c, m] = state[target, row + 3, c, m] + value

                    guarded(-1 if row < 0 else 1 if row > 5 else 0, run)

    def first_rows(cp, depth):
        wait_halo(cp, depth)
        low = -depth
        rows(3 * cp, 3 * cp + 1, low, 5 - 2 * low, 2, False)

    def ocean_steps(cp):
        for c in range(2):
            for q in range(nx):
                blocks = [gather_f[cp, side, q, c] for side in range(3)]
                force[c, :, q * quarter : (q + 1) * quarter] = stack_rows(*blocks)
        for _ in range(2):
            for c in range(2):
                here = ocean[c]
                lap = (
                    pltpu.roll(here, lon - 1, 1) + pltpu.roll(here, 1, 1)
                    + pltpu.roll(here, 15, 0) + pltpu.roll(here, 1, 0) - 4.0 * here
                )
                rate = visc[...] if c == 1 else OCEAN_DIFFUSION
                ocean[c] = here + mask[...] * (OCEAN_GAIN * force[c] + rate * lap)

    def send_x(cp, step):
        to = lax.rem(x + step, nx)
        return pltpu.make_async_remote_copy(
            part.at[cp, to], gather_x.at[cp, step - 1], x_send.at[cp, step - 1], x_recv.at[cp, step - 1],
            device_id=(yh * nx + to, lat), device_id_type=MESH,
        )

    def send_y(cp):
        return pltpu.make_async_remote_copy(
            total.at[cp], gather_y.at[cp], y_send.at[cp], y_recv.at[cp], device_id=partner, device_id_type=MESH
        )

    def send_f(cp, side, step, device):
        return pltpu.make_async_remote_copy(
            gather_f.at[cp, 1, x], gather_f.at[cp, 1 - side, x], f_send.at[cp, side + 1, step],
            f_recv.at[cp, side + 1, step], device_id=device, device_id_type=MESH,
        )

    def flux(cp):
        last = 3 * cp + 3
        count = lon // LANES
        for c in range(2):
            weights = [tiles(exv[c][m], count) for m in range(2)]
            own = pltpu.roll(ocean[c], 12, 0)[0:8]
            value = jnp.zeros((8, lon), F32)
            for row in range(6):
                line = weights[0] * state[last, row + 3, c, 0] + weights[1] * state[last, row + 3, c, 1]
                value = value + (pltpu.roll(line, row, 0) if row else line)
            value = value - (exc[c][0] + exc[c][1]) * own
            for q in range(nx):
                part[cp, q, c] = value[:, q * quarter : (q + 1) * quarter]

    def stage_y(cp):
        for step in range(1, nx):
            send_x(cp, step).wait_recv()
        total[cp] = (part[cp, x] + gather_x[cp, 0]) + (gather_x[cp, 1] + gather_x[cp, 2])
        send_y(cp).start()

    def stage_f(cp):
        send_y(cp).wait_recv()
        gather_f[cp, 1, x] = (total[cp] + gather_y[cp]) * scale
        for side, step, device in peers():
            guarded(side, lambda a=(side, step, device): send_f(cp, *a).start())

    def wait_f(cp):
        for side, step, device in peers():
            guarded(-side, lambda a=(side, step, device): send_f(cp, *a).wait_recv())

    for load in loads:
        load.wait()
    rows(0, 1, 1, 1, 4, False)
    pair.wait_recv()
    for side, step, device in peers():
        guarded(side, lambda a=(side, step, device): spread(1, *a).start())
    for depth in range(3):
        first_rows(0, depth)
    for stage in range(2):
        for side, step, device in peers():
            guarded(-side, lambda a=(stage, side, step, device): spread(*a).wait_recv())
    for field in range(3):
        for q in range(nx):
            blocks = []
            for side in range(3):
                even = chunks[(2 * q) // nx, side, (2 * q) % nx, field]
                odd = chunks[(2 * q + 1) // nx, side, (2 * q + 1) % nx, field]
                blocks.append(join_chunks(even, odd))
            value = stack_rows(*blocks)
            columns = slice(q * quarter, (q + 1) * quarter)
            if field == 2:
                visc[:, columns] = value
            else:
                ocean[field, :, columns] = value
    add_surface(1)
    rows(1, 2, -1, 1, 8, True)
    rows(2, 3, 0, 1, 6, True)
    flux(0)
    for step in range(1, nx):
        send_x(0, step).start()
    start_halos(1)
    rows(3, 4, 1, 1, 4, False)
    stage_y(0)
    first_rows(1, 0)
    first_rows(1, 1)
    stage_f(0)
    first_rows(1, 2)
    for side in (-1, 1):
        guarded(-side, lambda side=side: send_mask(side).wait_recv())
    mask[...] = stack_rows(masks[0], masks[1], masks[2])
    wait_f(0)
    ocean_steps(0)

    add_surface(4)
    rows(4, 5, -1, 1, 8, True)
    rows(5, 6, 0, 1, 6, True)
    flux(1)
    for step in range(1, nx):
        send_x(1, step).start()
    stores = [pltpu.make_async_copy(state.at[6, r + 3], atm_out.at[:, :, r], out_sem.at[r]) for r in range(6)]
    for store in stores:
        store.start()
    stage_y(1)
    stage_f(1)
    wait_f(1)
    ocean_steps(1)
    start = pl.multiple_of(((3 * me) // 2) * LANES, LANES)
    odd = lax.rem(me, 2) == 1
    for c in range(2):
        value = ocean[c, :, pl.ds(start, 2 * LANES)]
        value = jnp.where(odd, pltpu.roll(value, 192, 1), value)
        for r in range(6):
            ocean_out[r, c : c + 1, :] = value[r + 4 : r + 5, 0:192]

    for store in stores:
        store.wait()
    pair.wait_send()
    for side in (-1, 1):
        guarded(side, lambda side=side: send_mask(side).wait_send())
        for cp in range(2):
            for depth in range(3):
                guarded(side, lambda a=(cp, side, depth): halo(*a).wait_send())
    for stage in range(2):
        for side, step, device in peers():
            guarded(side, lambda a=(stage, side, step, device): spread(*a).wait_send())
    for cp in range(2):
        send_y(cp).wait_send()
        for step in range(1, nx):
            send_x(cp, step).wait_send()
        for side, step, device in peers():
            guarded(side, lambda a=(cp, side, step, device): send_f(*a).wait_send())


def body(nx, nlat, atmosphere, ocean_state, viscosity, sea_mask, parameter_index, parameter_table, level_mix):
    lon = atmosphere.shape[4]
    quarter = lon // nx
    vmem = pl.BlockSpec(memory_space=pltpu.VMEM)
    smem = pl.BlockSpec(memory_space=pltpu.SMEM)
    hbm = pl.BlockSpec(memory_space=pl.ANY)
    dma = pltpu.SemaphoreType.DMA
    fields = jnp.transpose(atmosphere, (0, 1, 3, 2, 4))
    atm_out, ocean_out = pl.pallas_call(
        functools.partial(kernel, nx, nlat, 1.0 / (4 * nx)),
        out_shape=(
            jax.ShapeDtypeStruct(fields.shape, F32),
            jax.ShapeDtypeStruct((6, 2, 192), F32),
        ),
        in_specs=[hbm, vmem, vmem, vmem, smem, smem, vmem],
        out_specs=(hbm, vmem),
        scratch_shapes=[
            pltpu.VMEM((7, 12, 2, 2, 8, lon), F32),
            pltpu.VMEM((2, 2, 8, 8, LANES), F32),
            pltpu.VMEM((2, 2, 8, LANES), F32),
            pltpu.VMEM((10, 2, 2, 8, lon), F32),
            pltpu.VMEM((2, 3, nx, 3, 8, 2 * LANES), F32),
            pltpu.VMEM((3, 8, lon), F32),
            pltpu.VMEM((2, 16, lon), F32),
            pltpu.VMEM((16, lon), F32),
            pltpu.VMEM((16, lon), F32),
            pltpu.VMEM((2, 16, lon), F32),
            pltpu.VMEM((2, nx, 2, 8, quarter), F32),
            pltpu.VMEM((2, nx - 1, 2, 8, quarter), F32),
            pltpu.VMEM((2, 2, 8, quarter), F32),
            pltpu.VMEM((2, 2, 8, quarter), F32),
            pltpu.VMEM((2, 3, nx, 2, 8, quarter), F32),
            pltpu.VMEM((3, 8, 2 * LANES), F32),
            dma((6,)),
            dma((2, 2, 3)),
            dma((2, 2, 3)),
            dma((2, 3, nx)),
            dma((2, 3, nx)),
            dma(()),
            dma(()),
            dma((2,)),
            dma((2,)),
            dma((2, nx - 1)),
            dma((2, nx - 1)),
            dma((2,)),
            dma((2,)),
            dma((2, 3, nx)),
            dma((2, 3, nx)),
            dma((6,)),
        ],
        compiler_params=pltpu.CompilerParams(
            collective_id=0, has_side_effects=True, vmem_limit_bytes=48 * 1024 * 1024
        ),
        name="coupled_window",
    )(
        fields,
        jnp.transpose(ocean_state, (1, 0, 2)),
        viscosity,
        sea_mask,
        parameter_index,
        jnp.transpose(parameter_table),
        level_mix,
    )
    return jnp.transpose(atm_out, (0, 1, 3, 2, 4)), jnp.transpose(ocean_out, (1, 0, 2))


def solution(mesh):
    return jax.shard_map(
        functools.partial(body, mesh.shape["member"] // 2, mesh.shape["lat"]),
        mesh=mesh,
        in_specs=(
            P(None, "member", None, "lat", None),
            P(None, "lat", "member"),
            P("lat", "member"),
            P("lat", None),
            P("member"),
            P(),
            P(),
        ),
        out_specs=(P(None, "member", None, "lat", None), P(None, "lat", "member")),
        check_vma=False,
    )
```

```python
import functools

import jax
import jax.numpy as jnp
from jax import lax
from jax.experimental import pallas as pl
from jax.experimental.pallas import tpu as pltpu
from jax.sharding import PartitionSpec as P

ADVECTION = 0.1
OCEAN_GAIN = 0.5
OCEAN_DIFFUSION = 0.15
MESH = pl.DeviceIdType.MESH
F32 = jnp.float32
LANES = 128
CHUNK = 512


def tiles(vector, count):
    return jnp.concatenate([vector] * count, axis=1)


def sublane(shape):
    return lax.broadcasted_iota(jnp.int32, shape, 0)


def stack_rows(south, own, north):
    index = sublane(own.shape)
    middle = pltpu.roll(own, 4, 0)
    low = jnp.where(index < 4, pltpu.roll(south, 6, 0), middle)
    high = jnp.where(index < 2, middle, pltpu.roll(north, 2, 0))
    return jnp.concatenate([low, high], axis=0)


def join_chunks(even, odd):
    lane = lax.broadcasted_iota(jnp.int32, (8, LANES), 1)
    first = pltpu.roll(odd[:, :LANES], 64, 1)
    second = pltpu.roll(odd[:, LANES:], 64, 1)
    return jnp.concatenate(
        [even[:, :LANES], jnp.where(lane < 64, even[:, LANES:], first), jnp.where(lane < 64, first, second)], axis=1
    )


def kernel(
    nx, nlat, scale,
    atm, ocean_hbm, visc_hbm, mask_hbm, pick_hbm, table_hbm, mixing_hbm, atm_out, ocean_out,
    ocean_in, visc_in, mask_in, pick, table, mixing,
    state, coef, diff, surf, chunks, masks, ocean, visc, mask, force, part, gather_x, total, gather_y, gather_f, seg,
    load_sem, halo_send, halo_recv, seg_send, seg_recv, pair_send, pair_recv, mask_send, mask_recv,
    x_send, x_recv, y_send, y_recv, f_send, f_recv, out_sem, small_sem,
):
    me = lax.axis_index("member")
    lat = lax.axis_index("lat")
    x, yh = lax.rem(me, nx), lax.div(me, nx)
    has_south, has_north = lat > 0, lat < nlat - 1
    partner = ((1 - yh) * nx + x, lat)
    lon = mask_in.shape[1]
    pieces = lon // CHUNK
    quarter = lon // nx

    def peers():
        for side in (-1, 0, 1):
            for step in range(nx):
                if side or step:
                    yield side, step, (yh * nx + lax.rem(x + step, nx), lat + side)

    def guarded(side, run):
        if side < 0:
            pl.when(has_south)(run)
        elif side > 0:
            pl.when(has_north)(run)
        else:
            run()

    loads = [pltpu.make_async_copy(atm.at[:, :, r], state.at[0, r + 3], load_sem.at[r]) for r in range(6)]
    small = [
        pltpu.make_async_copy(source, target, small_sem.at[i])
        for i, (source, target) in enumerate(
            (
                (ocean_hbm, ocean_in), (visc_hbm, visc_in), (mask_hbm, mask_in),
                (pick_hbm, pick), (table_hbm, table), (mixing_hbm, mixing),
            )
        )
    ]
    for load in small:
        load.start()
    for load in loads:
        load.start()

    barrier = pltpu.get_barrier_semaphore()
    pl.semaphore_signal(barrier, inc=1, device_id=partner, device_id_type=MESH)
    for side, step, device in peers():
        guarded(side, lambda device=device: pl.semaphore_signal(barrier, inc=1, device_id=device, device_id_type=MESH))

    for load in small:
        load.wait()

    lane_pad = jnp.zeros((8, 2 * LANES), F32)
    for field in range(3):
        seg[field] = lane_pad
        for r in range(6):
            line = visc_in[r : r + 1, :] if field == 2 else ocean_in[r, field : field + 1, :]
            seg[field, r : r + 1, 0:192] = line
    masks[1] = jnp.zeros((8, lon), F32)
    masks[1, 0:6, :] = mask_in[...].astype(F32)
    row_zero = jnp.zeros((2, 2, 8, lon), F32)

    @pl.when(lat == 0)
    def _():
        for b in range(6):
            state[b, 2] = row_zero
        masks[0] = jnp.zeros((8, lon), F32)
        for a in range(2):
            for i in range(nx):
                chunks[a, 0, i] = jnp.zeros((3, 8, 2 * LANES), F32)
                gather_f[a, 0, i] = jnp.zeros((2, 8, quarter), F32)

    @pl.when(lat == nlat - 1)
    def _():
        for b in range(6):
            state[b, 9] = row_zero
        masks[2] = jnp.zeros((8, lon), F32)
        for a in range(2):
            for i in range(nx):
                chunks[a, 2, i] = jnp.zeros((3, 8, 2 * LANES), F32)
                gather_f[a, 2, i] = jnp.zeros((2, 8, quarter), F32)

    pl.semaphore_wait(barrier, nx + nx * has_south.astype(jnp.int32) + nx * has_north.astype(jnp.int32))

    def halo(cp, side, depth):
        row = 5 - depth if side > 0 else depth
        there = 2 - depth if side > 0 else 9 + depth
        source = atm.at[:, :, row] if cp == 0 else state.at[3, row + 3]
        k = (side + 1) // 2
        return pltpu.make_async_remote_copy(
            source, state.at[3 * cp, there], halo_send.at[cp, k, depth], halo_recv.at[cp, k, depth],
            device_id=(me, lat + side), device_id_type=MESH,
        )

    def start_halos(cp):
        for depth in range(3):
            for side in (-1, 1):
                guarded(side, lambda side=side, depth=depth: halo(cp, side, depth).start())

    def wait_halo(cp, depth):
        for side in (-1, 1):
            guarded(-side, lambda side=side: halo(cp, side, depth).wait_recv())

    def spread(stage, side, step, device):
        source = seg if stage == 0 else chunks.at[1 - yh, 1, x]
        target = chunks.at[yh if stage == 0 else 1 - yh, 1 - side, x]
        return pltpu.make_async_remote_copy(
            source, target, seg_send.at[stage, side + 1, step], seg_recv.at[stage, side + 1, step],
            device_id=device, device_id_type=MESH,
        )

    pair = pltpu.make_async_remote_copy(
        seg, chunks.at[yh, 1, x], pair_send, pair_recv, device_id=partner, device_id_type=MESH
    )

    def send_mask(side):
        return pltpu.make_async_remote_copy(
            masks.at[1], masks.at[1 - side], mask_send.at[(side + 1) // 2], mask_recv.at[(side + 1) // 2],
            device_id=(me, lat + side), device_id_type=MESH,
        )

    pair.start()
    start_halos(0)
    for side, step, device in peers():
        guarded(side, lambda a=(side, step, device): spread(0, *a).start())
    for side in (-1, 1):
        guarded(side, lambda side=side: send_mask(side).start())
    chunks[yh, 1, x] = seg[...]

    sub = sublane((8, LANES))
    top = sub == 0
    dif = [0.6 * table[0, pick[m]] for m in range(2)]
    exc = [[2.0 * table[1 + c, pick[m]] for m in range(2)] for c in range(2)]
    exv = [[jnp.where(top, exc[c][m], 0.0) for m in range(2)] for c in range(2)]
    mix = mixing[...]
    row8 = lax.broadcasted_iota(jnp.int32, (8, 8), 0)
    col8 = lax.broadcasted_iota(jnp.int32, (8, 8), 1)
    for m in range(2):
        diff[m, 0] = jnp.full((8, LANES), dif[m], F32)
        diff[m, 1] = jnp.full((8, LANES), 1.0 - 4.0 * dif[m], F32) / diff[m, 0]
        diff[m, 0] = (0.5 * ADVECTION) / diff[m, 0]
    for r in range(8):
        diagonal = jnp.sum(jnp.where(col8 == lax.rem(row8 - r + 8, 8), mix, 0.0), axis=1, keepdims=True)
        value = jnp.broadcast_to(diagonal, (8, LANES))
        if r == 0:
            value = value + 1.0
        for c in range(2):
            for m in range(2):
                weight = dif[m] * jnp.where(top, value * (1.0 - exc[c][m]), value)
                coef[c, m, r] = pltpu.roll(weight, 4, 0) if r >= 4 else weight

    def unit(source, target, e, m, k, with_surface):
        width = CHUNK // LANES
        off, right, left = k * CHUNK, (k + 1) % pieces * CHUNK, (k * CHUNK - LANES) % lon
        gain = tiles(diff[m, 0], width)
        keep = tiles(diff[m, 1], width)
        wind = None
        for c in (1, 0):
            centre = state[source, e, c, m, :, off : off + CHUNK]
            ahead = state[source, e, c, m, :, right : right + LANES]
            behind = state[source, e, c, m, :, left : left + LANES]
            north = state[source, e + 1, c, m, :, off : off + CHUNK]
            south = state[source, e - 1, c, m, :, off : off + CHUNK]
            east = pltpu.roll(jnp.concatenate([centre, ahead], axis=1), CHUNK + LANES - 1, 1)[:, :CHUNK]
            west = pltpu.roll(jnp.concatenate([centre, behind], axis=1), 1, 1)[:, :CHUNK]
            if c == 1:
                wind = gain * centre
            advected = keep * centre + ((east + west) + (north + south)) - wind * (east - west)
            near = tiles(coef[c, m, 0], width) * advected
            far = tiles(coef[c, m, 4], width) * advected
            for r in range(1, 4):
                turned = pltpu.roll(advected, r, 0)
                near = near + tiles(coef[c, m, r], width) * turned
                far = far + tiles(coef[c, m, r + 4], width) * turned
            value = near + pltpu.roll(far, 4, 0)
            if with_surface:
                value = value + surf[e - 1, c, m, :, off : off + CHUNK]
            state[target, e, c, m, :, off : off + CHUNK] = value

    def rows(source, target, first, stride, count, with_surface):
        def body(i, carry):
            row = first + i * stride
            inside = ((row >= 0) | has_south) & ((row <= 5) | has_north)

            @pl.when(inside)
            def _():
                for m in range(2):
                    for k in range(pieces):
                        unit(source, target, row + 3, m, k, with_surface)

            return carry

        lax.fori_loop(0, count, body, 0)

    def add_surface(target):
        for row in range(-2, 8):
            for c in range(2):
                line = jnp.broadcast_to(ocean[c, row + 4 : row + 5, :], (8, lon))
                for m in range(2):
                    value = tiles(exv[c][m], lon // LANES) * line
                    surf[row + 2, c, m] = value

                    def run(value=value, c=c, m=m, row=row):
                        state[target, row + 3, c, m] = state[target, row + 3, c, m] + value

                    guarded(-1 if row < 0 else 1 if row > 5 else 0, run)

    def first_rows(cp, depth):
        wait_halo(cp, depth)
        low = -depth
        rows(3 * cp, 3 * cp + 1, low, 5 - 2 * low, 2, False)

    def ocean_steps(cp):
        for c in range(2):
            for q in range(nx):
                blocks = [gather_f[cp, side, q, c] for side in range(3)]
                force[c, :, q * quarter : (q + 1) * quarter] = stack_rows(*blocks)
        for _ in range(2):
            for c in range(2):
                here = ocean[c]
                lap = (
                    pltpu.roll(here, lon - 1, 1) + pltpu.roll(here, 1, 1)
                    + pltpu.roll(here, 15, 0) + pltpu.roll(here, 1, 0) - 4.0 * here
                )
                rate = visc[...] if c == 1 else OCEAN_DIFFUSION
                ocean[c] = here + mask[...] * (OCEAN_GAIN * force[c] + rate * lap)

    def send_x(cp, step):
        to = lax.rem(x + step, nx)
        return pltpu.make_async_remote_copy(
            part.at[cp, to], gather_x.at[cp, step - 1], x_send.at[cp, step - 1], x_recv.at[cp, step - 1],
            device_id=(yh * nx + to, lat), device_id_type=MESH,
        )

    def send_y(cp):
        return pltpu.make_async_remote_copy(
            total.at[cp], gather_y.at[cp], y_send.at[cp], y_recv.at[cp], device_id=partner, device_id_type=MESH
        )

    def send_f(cp, side, step, device):
        return pltpu.make_async_remote_copy(
            gather_f.at[cp, 1, x], gather_f.at[cp, 1 - side, x], f_send.at[cp, side + 1, step],
            f_recv.at[cp, side + 1, step], device_id=device, device_id_type=MESH,
        )

    def flux(cp):
        last = 3 * cp + 3
        count = lon // LANES
        for c in range(2):
            weights = [tiles(exv[c][m], count) for m in range(2)]
            own = pltpu.roll(ocean[c], 12, 0)[0:8]
            value = jnp.zeros((8, lon), F32)
            for row in range(6):
                line = weights[0] * state[last, row + 3, c, 0] + weights[1] * state[last, row + 3, c, 1]
                value = value + (pltpu.roll(line, row, 0) if row else line)
            value = value - (exc[c][0] + exc[c][1]) * own
            for q in range(nx):
                part[cp, q, c] = value[:, q * quarter : (q + 1) * quarter]

    def stage_y(cp):
        for step in range(1, nx):
            send_x(cp, step).wait_recv()
        total[cp] = (part[cp, x] + gather_x[cp, 0]) + (gather_x[cp, 1] + gather_x[cp, 2])
        send_y(cp).start()

    def stage_f(cp):
        send_y(cp).wait_recv()
        gather_f[cp, 1, x] = (total[cp] + gather_y[cp]) * scale
        for side, step, device in peers():
            guarded(side, lambda a=(side, step, device): send_f(cp, *a).start())

    def wait_f(cp):
        for side, step, device in peers():
            guarded(-side, lambda a=(side, step, device): send_f(cp, *a).wait_recv())

    for load in loads:
        load.wait()
    rows(0, 1, 1, 1, 4, False)
    pair.wait_recv()
    for side, step, device in peers():
        guarded(side, lambda a=(side, step, device): spread(1, *a).start())
    for depth in range(3):
        first_rows(0, depth)
    for stage in range(2):
        for side, step, device in peers():
            guarded(-side, lambda a=(stage, side, step, device): spread(*a).wait_recv())
    for field in range(3):
        for q in range(nx):
            blocks = []
            for side in range(3):
                even = chunks[(2 * q) // nx, side, (2 * q) % nx, field]
                odd = chunks[(2 * q + 1) // nx, side, (2 * q + 1) % nx, field]
                blocks.append(join_chunks(even, odd))
            value = stack_rows(*blocks)
            columns = slice(q * quarter, (q + 1) * quarter)
            if field == 2:
                visc[:, columns] = value
            else:
                ocean[field, :, columns] = value
    add_surface(1)
    rows(1, 2, -1, 1, 8, True)
    rows(2, 3, 0, 1, 6, True)
    flux(0)
    for step in range(1, nx):
        send_x(0, step).start()
    start_halos(1)
    rows(3, 4, 1, 1, 4, False)
    stage_y(0)
    first_rows(1, 0)
    first_rows(1, 1)
    stage_f(0)
    first_rows(1, 2)
    for side in (-1, 1):
        guarded(-side, lambda side=side: send_mask(side).wait_recv())
    mask[...] = stack_rows(masks[0], masks[1], masks[2])
    wait_f(0)
    ocean_steps(0)

    add_surface(4)
    rows(4, 5, -1, 1, 8, True)
    rows(5, 6, 0, 1, 6, True)
    flux(1)
    for step in range(1, nx):
        send_x(1, step).start()
    stores = [pltpu.make_async_copy(state.at[6, r + 3], atm_out.at[:, :, r], out_sem.at[r]) for r in range(6)]
    for store in stores:
        store.start()
    stage_y(1)
    stage_f(1)
    wait_f(1)
    ocean_steps(1)
    start = pl.multiple_of(((3 * me) // 2) * LANES, LANES)
    odd = lax.rem(me, 2) == 1
    for c in range(2):
        value = ocean[c, :, pl.ds(start, 2 * LANES)]
        value = jnp.where(odd, pltpu.roll(value, 192, 1), value)
        for r in range(6):
            ocean_out[r, c : c + 1, :] = value[r + 4 : r + 5, 0:192]

    for store in stores:
        store.wait()
    pair.wait_send()
    for side in (-1, 1):
        guarded(side, lambda side=side: send_mask(side).wait_send())
        for cp in range(2):
            for depth in range(3):
                guarded(side, lambda a=(cp, side, depth): halo(*a).wait_send())
    for stage in range(2):
        for side, step, device in peers():
            guarded(side, lambda a=(stage, side, step, device): spread(*a).wait_send())
    for cp in range(2):
        send_y(cp).wait_send()
        for step in range(1, nx):
            send_x(cp, step).wait_send()
        for side, step, device in peers():
            guarded(side, lambda a=(cp, side, step, device): send_f(*a).wait_send())


def body(nx, nlat, atmosphere, ocean_state, viscosity, sea_mask, parameter_index, parameter_table, level_mix):
    lon = atmosphere.shape[4]
    quarter = lon // nx
    vmem = pl.BlockSpec(memory_space=pltpu.VMEM)
    hbm = pl.BlockSpec(memory_space=pl.ANY)
    dma = pltpu.SemaphoreType.DMA
    fields = jnp.transpose(atmosphere, (0, 1, 3, 2, 4))
    atm_out, ocean_out = pl.pallas_call(
        functools.partial(kernel, nx, nlat, 1.0 / (4 * nx)),
        out_shape=(
            jax.ShapeDtypeStruct(fields.shape, F32),
            jax.ShapeDtypeStruct((6, 2, 192), F32),
        ),
        in_specs=[hbm] * 7,
        out_specs=(hbm, vmem),
        scratch_shapes=[
            pltpu.VMEM((6, 2, 192), F32),
            pltpu.VMEM((6, 192), F32),
            pltpu.VMEM((6, lon), jnp.int32),
            pltpu.SMEM((2,), jnp.int32),
            pltpu.SMEM(parameter_table.shape[::-1], F32),
            pltpu.VMEM((8, 8), F32),
            pltpu.VMEM((7, 12, 2, 2, 8, lon), F32),
            pltpu.VMEM((2, 2, 8, 8, LANES), F32),
            pltpu.VMEM((2, 2, 8, LANES), F32),
            pltpu.VMEM((10, 2, 2, 8, lon), F32),
            pltpu.VMEM((2, 3, nx, 3, 8, 2 * LANES), F32),
            pltpu.VMEM((3, 8, lon), F32),
            pltpu.VMEM((2, 16, lon), F32),
            pltpu.VMEM((16, lon), F32),
            pltpu.VMEM((16, lon), F32),
            pltpu.VMEM((2, 16, lon), F32),
            pltpu.VMEM((2, nx, 2, 8, quarter), F32),
            pltpu.VMEM((2, nx - 1, 2, 8, quarter), F32),
            pltpu.VMEM((2, 2, 8, quarter), F32),
            pltpu.VMEM((2, 2, 8, quarter), F32),
            pltpu.VMEM((2, 3, nx, 2, 8, quarter), F32),
            pltpu.VMEM((3, 8, 2 * LANES), F32),
            dma((6,)),
            dma((2, 2, 3)),
            dma((2, 2, 3)),
            dma((2, 3, nx)),
            dma((2, 3, nx)),
            dma(()),
            dma(()),
            dma((2,)),
            dma((2,)),
            dma((2, nx - 1)),
            dma((2, nx - 1)),
            dma((2,)),
            dma((2,)),
            dma((2, 3, nx)),
            dma((2, 3, nx)),
            dma((6,)),
            dma((6,)),
        ],
        compiler_params=pltpu.CompilerParams(
            collective_id=0, has_side_effects=True, vmem_limit_bytes=67043328
        ),
        name="coupled_window",
    )(
        fields,
        jnp.transpose(ocean_state, (1, 0, 2)),
        viscosity,
        sea_mask,
        parameter_index,
        jnp.transpose(parameter_table),
        level_mix,
    )
    return jnp.transpose(atm_out, (0, 1, 3, 2, 4)), jnp.transpose(ocean_out, (1, 0, 2))


def solution(mesh):
    return jax.shard_map(
        functools.partial(body, mesh.shape["member"] // 2, mesh.shape["lat"]),
        mesh=mesh,
        in_specs=(
            P(None, "member", None, "lat", None),
            P(None, "lat", "member"),
            P("lat", "member"),
            P("lat", None),
            P("member"),
            P(),
            P(),
        ),
        out_specs=(P(None, "member", None, "lat", None), P(None, "lat", "member")),
        check_vma=False,
    )
```

```python
import functools

import jax
import jax.numpy as jnp
from jax import lax
from jax.experimental import pallas as pl
from jax.experimental.pallas import tpu as pltpu
from jax.sharding import PartitionSpec as P

ADVECTION = 0.1
OCEAN_GAIN = 0.5
OCEAN_DIFFUSION = 0.15
MESH = pl.DeviceIdType.MESH
F32 = jnp.float32
LANES = 128
CHUNK = 512


def tiles(vector, count):
    return jnp.concatenate([vector] * count, axis=1)


def sublane(shape):
    return lax.broadcasted_iota(jnp.int32, shape, 0)


def stack_rows(south, own, north):
    index = sublane(own.shape)
    middle = pltpu.roll(own, 4, 0)
    low = jnp.where(index < 4, pltpu.roll(south, 6, 0), middle)
    high = jnp.where(index < 2, middle, pltpu.roll(north, 2, 0))
    return jnp.concatenate([low, high], axis=0)


def join_chunks(even, odd):
    lane = lax.broadcasted_iota(jnp.int32, (8, LANES), 1)
    first = pltpu.roll(odd[:, :LANES], 64, 1)
    second = pltpu.roll(odd[:, LANES:], 64, 1)
    return jnp.concatenate(
        [even[:, :LANES], jnp.where(lane < 64, even[:, LANES:], first), jnp.where(lane < 64, first, second)], axis=1
    )


def kernel(
    nx, nlat, scale,
    atm, ocean_hbm, visc_hbm, mask_hbm, pick_hbm, table_hbm, mixing_hbm, atm_out, ocean_out,
    ocean_in, visc_in, mask_in, pick, table, mixing,
    state, coef, diff, surf, chunks, masks, ocean, visc, mask, force, part, gather_r, gather_f, gather_l, seg,
    load_sem, halo_send, halo_recv, seg_send, seg_recv, pair_send, pair_recv, mask_send, mask_recv,
    r_send, r_recv, f_send, f_recv, l_send, l_recv, small_sem,
):
    me = lax.axis_index("member")
    lat = lax.axis_index("lat")
    x, yh = lax.rem(me, nx), lax.div(me, nx)
    has_south, has_north = lat > 0, lat < nlat - 1
    partner = ((1 - yh) * nx + x, lat)
    lon = mask_in.shape[1]
    pieces = lon // CHUNK
    quarter = lon // nx
    columns = lon // LANES
    window = quarter // LANES
    members = 2 * nx

    def peers():
        for side in (-1, 0, 1):
            for step in range(nx):
                if side or step:
                    yield side, step, (yh * nx + lax.rem(x + step, nx), lat + side)

    def guarded(side, run):
        if side < 0:
            pl.when(has_south)(run)
        elif side > 0:
            pl.when(has_north)(run)
        else:
            run()

    loads = [pltpu.make_async_copy(atm.at[:, :, r], state.at[0, r + 3], load_sem.at[r]) for r in range(6)]
    small = [
        pltpu.make_async_copy(source, target, small_sem.at[i])
        for i, (source, target) in enumerate(
            (
                (ocean_hbm, ocean_in), (visc_hbm, visc_in), (mask_hbm, mask_in),
                (pick_hbm, pick), (table_hbm, table), (mixing_hbm, mixing),
            )
        )
    ]
    for load in small:
        load.start()
    for load in loads:
        load.start()

    barrier = pltpu.get_barrier_semaphore()
    for step in range(1, members):
        device = (lax.rem(me + step, members), lat)
        pl.semaphore_signal(barrier, inc=1, device_id=device, device_id_type=MESH)
    for side, step, device in peers():
        if side:
            guarded(side, lambda device=device: pl.semaphore_signal(barrier, inc=1, device_id=device, device_id_type=MESH))

    for load in small:
        load.wait()

    lane_pad = jnp.zeros((8, 2 * LANES), F32)
    for field in range(3):
        seg[field] = lane_pad
        for r in range(6):
            line = visc_in[r : r + 1, :] if field == 2 else ocean_in[r, field : field + 1, :]
            seg[field, r : r + 1, 0:192] = line
    masks[1] = jnp.zeros((8, lon), F32)
    masks[1, 0:6, :] = mask_in[...].astype(F32)
    row_zero = jnp.zeros((2, 2, 8, lon), F32)

    @pl.when(lat == 0)
    def _():
        for b in range(6):
            state[b, 2] = row_zero
        masks[0] = jnp.zeros((8, lon), F32)
        gather_l[0] = jnp.zeros((window, 2, 8, LANES), F32)
        for i in range(nx):
            gather_f[0, i] = jnp.zeros((window, 2, 8, LANES), F32)
            for a in range(2):
                chunks[a, 0, i] = jnp.zeros((3, 8, 2 * LANES), F32)

    @pl.when(lat == nlat - 1)
    def _():
        for b in range(6):
            state[b, 9] = row_zero
        masks[2] = jnp.zeros((8, lon), F32)
        gather_l[2] = jnp.zeros((window, 2, 8, LANES), F32)
        for i in range(nx):
            gather_f[2, i] = jnp.zeros((window, 2, 8, LANES), F32)
            for a in range(2):
                chunks[a, 2, i] = jnp.zeros((3, 8, 2 * LANES), F32)

    pl.semaphore_wait(barrier, members - 1 + nx * has_south.astype(jnp.int32) + nx * has_north.astype(jnp.int32))

    def halo(cp, side, depth):
        row = 5 - depth if side > 0 else depth
        there = 2 - depth if side > 0 else 9 + depth
        source = atm.at[:, :, row] if cp == 0 else state.at[3, row + 3]
        k = (side + 1) // 2
        return pltpu.make_async_remote_copy(
            source, state.at[3 * cp, there], halo_send.at[cp, k, depth], halo_recv.at[cp, k, depth],
            device_id=(me, lat + side), device_id_type=MESH,
        )

    def start_halos(cp, depths):
        for depth in depths:
            for side in (-1, 1):
                guarded(side, lambda side=side, depth=depth: halo(cp, side, depth).start())

    def wait_halo(cp, depth):
        for side in (-1, 1):
            guarded(-side, lambda side=side: halo(cp, side, depth).wait_recv())

    def spread(stage, side, step, device):
        source = seg if stage == 0 else chunks.at[1 - yh, 1, x]
        target = chunks.at[yh if stage == 0 else 1 - yh, 1 - side, x]
        return pltpu.make_async_remote_copy(
            source, target, seg_send.at[stage, side + 1, step], seg_recv.at[stage, side + 1, step],
            device_id=device, device_id_type=MESH,
        )

    pair = pltpu.make_async_remote_copy(
        seg, chunks.at[yh, 1, x], pair_send, pair_recv, device_id=partner, device_id_type=MESH
    )

    def send_mask(side):
        return pltpu.make_async_remote_copy(
            masks.at[1], masks.at[1 - side], mask_send.at[(side + 1) // 2], mask_recv.at[(side + 1) // 2],
            device_id=(me, lat + side), device_id_type=MESH,
        )

    pair.start()
    for side, step, device in peers():
        guarded(side, lambda a=(side, step, device): spread(0, *a).start())
    start_halos(0, (0, 1))
    chunks[yh, 1, x] = seg[...]

    sub = sublane((8, LANES))
    top = sub == 0
    dif = [0.6 * table[0, pick[m]] for m in range(2)]
    exc = [[2.0 * table[1 + c, pick[m]] for m in range(2)] for c in range(2)]
    exv = [[jnp.where(top, exc[c][m], 0.0) for m in range(2)] for c in range(2)]
    mix = mixing[...]
    row8 = lax.broadcasted_iota(jnp.int32, (8, 8), 0)
    col8 = lax.broadcasted_iota(jnp.int32, (8, 8), 1)
    for m in range(2):
        diff[m, 0] = jnp.full((8, LANES), dif[m], F32)
        diff[m, 1] = jnp.full((8, LANES), 1.0 - 4.0 * dif[m], F32) / diff[m, 0]
        diff[m, 0] = (0.5 * ADVECTION) / diff[m, 0]
    for r in range(8):
        diagonal = jnp.sum(jnp.where(col8 == lax.rem(row8 - r + 8, 8), mix, 0.0), axis=1, keepdims=True)
        value = jnp.broadcast_to(diagonal, (8, LANES))
        if r == 0:
            value = value + 1.0
        for c in range(2):
            for m in range(2):
                weight = dif[m] * jnp.where(top, value * (1.0 - exc[c][m]), value)
                coef[c, m, r] = pltpu.roll(weight, 4, 0) if r >= 4 else weight

    def unit(source, target, e, m, k, with_surface):
        width = CHUNK // LANES
        off, right, left = k * CHUNK, (k + 1) % pieces * CHUNK, (k * CHUNK - LANES) % lon
        gain = tiles(diff[m, 0], width)
        keep = tiles(diff[m, 1], width)
        wind = None
        for c in (1, 0):
            centre = state[source, e, c, m, :, off : off + CHUNK]
            ahead = state[source, e, c, m, :, right : right + LANES]
            behind = state[source, e, c, m, :, left : left + LANES]
            north = state[source, e + 1, c, m, :, off : off + CHUNK]
            south = state[source, e - 1, c, m, :, off : off + CHUNK]
            east = pltpu.roll(jnp.concatenate([centre, ahead], axis=1), CHUNK + LANES - 1, 1)[:, :CHUNK]
            west = pltpu.roll(jnp.concatenate([centre, behind], axis=1), 1, 1)[:, :CHUNK]
            if c == 1:
                wind = gain * centre
            advected = keep * centre + ((east + west) + (north + south)) - wind * (east - west)
            near = tiles(coef[c, m, 0], width) * advected
            far = tiles(coef[c, m, 4], width) * advected
            for r in range(1, 4):
                turned = pltpu.roll(advected, r, 0)
                near = near + tiles(coef[c, m, r], width) * turned
                far = far + tiles(coef[c, m, r + 4], width) * turned
            value = near + pltpu.roll(far, 4, 0)
            if with_surface:
                value = value + surf[e - 1, c, m, :, off : off + CHUNK]
            if target == 6:
                atm_out[c, m, e - 3, :, off : off + CHUNK] = value
            else:
                state[target, e, c, m, :, off : off + CHUNK] = value

    def rows(source, target, first, stride, count, with_surface):
        def body(i, carry):
            row = first + i * stride
            inside = ((row >= 0) | has_south) & ((row <= 5) | has_north)

            @pl.when(inside)
            def _():
                for m in range(2):
                    for k in range(pieces):
                        unit(source, target, row + 3, m, k, with_surface)

            return carry

        lax.fori_loop(0, count, body, 0)

    def add_surface(target):
        for row in range(-2, 8):
            for c in range(2):
                line = jnp.broadcast_to(ocean[c, row + 4 : row + 5, :], (8, lon))
                for m in range(2):
                    value = tiles(exv[c][m], lon // LANES) * line
                    surf[row + 2, c, m] = value

                    def run(value=value, c=c, m=m, row=row):
                        state[target, row + 3, c, m] = state[target, row + 3, c, m] + value

                    guarded(-1 if row < 0 else 1 if row > 5 else 0, run)

    def first_rows(cp, depth):
        wait_halo(cp, depth)
        low = -depth
        rows(3 * cp, 3 * cp + 1, low, 5 - 2 * low, 2, False)

    def advance(here, rate, sea, drive):
        width = here.shape[1]
        lap = (
            pltpu.roll(here, width - 1, 1) + pltpu.roll(here, 1, 1)
            + pltpu.roll(here, 15, 0) + pltpu.roll(here, 1, 0) - 4.0 * here
        )
        return here + sea * (OCEAN_GAIN * drive + rate * lap)

    def ocean_steps():
        for c in range(2):
            for q in range(nx):
                for j in range(window):
                    blocks = [gather_f[side, q, j, c] for side in range(3)]
                    start = q * quarter + j * LANES
                    force[c, :, start : start + LANES] = stack_rows(*blocks)
        for _ in range(2):
            for c in range(2):
                rate = visc[...] if c == 1 else OCEAN_DIFFUSION
                ocean[c] = advance(ocean[c], rate, mask[...], force[c])

    def first_tile(cp, member):
        if cp == 0:
            return window * lax.rem(member, nx)
        return lax.rem(lax.div(3 * member + 2 * columns - 1, 2), columns)

    def send_r(cp, step):
        to = lax.rem(me + step, members)
        return pltpu.make_async_remote_copy(
            part.at[cp, pl.ds(first_tile(cp, to), window)], gather_r.at[cp, step - 1],
            r_send.at[cp, step - 1], r_recv.at[cp, step - 1], device_id=(to, lat), device_id_type=MESH,
        )

    def send_f(side, step, device):
        return pltpu.make_async_remote_copy(
            gather_f.at[1, x], gather_f.at[1 - side, x], f_send.at[side + 1, step],
            f_recv.at[side + 1, step], device_id=device, device_id_type=MESH,
        )

    def send_l(side):
        k = (side + 1) // 2
        return pltpu.make_async_remote_copy(
            gather_l.at[1], gather_l.at[1 - side], l_send.at[k], l_recv.at[k],
            device_id=(me, lat + side), device_id_type=MESH,
        )

    def flux(cp):
        for c in range(2):
            weights = [tiles(exv[c][m], columns) for m in range(2)]
            own = pltpu.roll(ocean[c], 12, 0)[0:8]
            value = jnp.zeros((8, lon), F32)
            for row in range(6):
                last = [atm_out[c, m, row] if cp else state[3, row + 3, c, m] for m in range(2)]
                line = weights[0] * last[0] + weights[1] * last[1]
                value = value + (pltpu.roll(line, row, 0) if row else line)
            value = value - (exc[c][0] + exc[c][1]) * own
            for j in range(columns + 2):
                start = j % columns * LANES
                part[cp, j, c] = value[:, start : start + LANES]
        for step in range(1, members):
            send_r(cp, step).start()

    def total(cp):
        for step in range(1, members):
            send_r(cp, step).wait_recv()
        parts = [part[cp, pl.ds(first_tile(cp, me), window)]] + [gather_r[cp, k] for k in range(members - 1)]
        while len(parts) > 1:
            parts = [a + b for a, b in zip(parts[0::2], parts[1::2])]
        return parts[0] * scale

    for load in loads:
        load.wait()
    rows(0, 1, 1, 1, 4, False)
    pair.wait_recv()
    for side, step, device in peers():
        guarded(side, lambda a=(side, step, device): spread(1, *a).start())
    start_halos(0, (2,))
    for side in (-1, 1):
        guarded(side, lambda side=side: send_mask(side).start())
    for depth in range(3):
        first_rows(0, depth)
    for stage in range(2):
        for side, step, device in peers():
            guarded(-side, lambda a=(stage, side, step, device): spread(*a).wait_recv())
    for field in range(3):
        for q in range(nx):
            blocks = []
            for side in range(3):
                even = chunks[(2 * q) // nx, side, (2 * q) % nx, field]
                odd = chunks[(2 * q + 1) // nx, side, (2 * q + 1) % nx, field]
                blocks.append(join_chunks(even, odd))
            value = stack_rows(*blocks)
            span = slice(q * quarter, (q + 1) * quarter)
            if field == 2:
                visc[:, span] = value
            else:
                ocean[field, :, span] = value
    add_surface(1)
    rows(1, 2, -1, 1, 8, True)
    rows(2, 3, 0, 1, 6, True)
    flux(0)
    start_halos(1, range(3))
    rows(3, 4, 1, 1, 4, False)
    first_rows(1, 0)
    first_rows(1, 1)
    gather_f[1, x] = total(0)
    for side, step, device in peers():
        guarded(side, lambda a=(side, step, device): send_f(*a).start())
    first_rows(1, 2)
    for side in (-1, 1):
        guarded(-side, lambda side=side: send_mask(side).wait_recv())
    mask[...] = stack_rows(masks[0], masks[1], masks[2])
    for side, step, device in peers():
        guarded(-side, lambda a=(side, step, device): send_f(*a).wait_recv())
    ocean_steps()

    add_surface(4)
    rows(4, 5, -1, 1, 8, True)
    rows(5, 6, 0, 1, 6, True)
    flux(1)
    gather_l[1] = total(1)
    for side in (-1, 1):
        guarded(side, lambda side=side: send_l(side).start())
    starts = [pl.multiple_of(lax.rem(first_tile(1, me) + j, columns) * LANES, LANES) for j in range(window)]

    def windowed(ref, *lead):
        return jnp.concatenate([ref[(*lead, slice(None), pl.ds(start, LANES))] for start in starts], axis=1)

    here = [windowed(ocean, c) for c in range(2)]
    rates = [OCEAN_DIFFUSION, windowed(visc)]
    sea = windowed(mask)
    odd = lax.rem(me, 2) == 1
    for side in (-1, 1):
        guarded(-side, lambda side=side: send_l(side).wait_recv())
    for c in range(2):
        drive = jnp.concatenate(
            [stack_rows(*[gather_l[side, j, c] for side in range(3)]) for j in range(window)], axis=1
        )
        value = advance(advance(here[c], rates[c], sea, drive), rates[c], sea, drive)
        value = jnp.where(odd, pltpu.roll(value, 64, 1), value)
        for r in range(6):
            ocean_out[r, c : c + 1, :] = value[r + 4 : r + 5, LANES : LANES + 192]

    pair.wait_send()
    for side in (-1, 1):
        guarded(side, lambda side=side: send_mask(side).wait_send())
        guarded(side, lambda side=side: send_l(side).wait_send())
        for cp in range(2):
            for depth in range(3):
                guarded(side, lambda a=(cp, side, depth): halo(*a).wait_send())
    for stage in range(2):
        for side, step, device in peers():
            guarded(side, lambda a=(stage, side, step, device): spread(*a).wait_send())
    for cp in range(2):
        for step in range(1, members):
            send_r(cp, step).wait_send()
    for side, step, device in peers():
        guarded(side, lambda a=(side, step, device): send_f(*a).wait_send())


def store(atm, ocean, atm_out, ocean_out, sem):
    copies = [pltpu.make_async_copy(ocean, ocean_out, sem.at[4])]
    copies += [pltpu.make_async_copy(atm.at[c, m], atm_out.at[c, m], sem.at[2 * c + m]) for c in range(2) for m in range(2)]
    for copy in copies:
        copy.start()
    for copy in copies:
        copy.wait()


def body(nx, nlat, atmosphere, ocean_state, viscosity, sea_mask, parameter_index, parameter_table, level_mix):
    lon = atmosphere.shape[4]
    quarter = lon // nx
    vmem = pl.BlockSpec(memory_space=pltpu.VMEM)
    hbm = pl.BlockSpec(memory_space=pltpu.HBM)
    anywhere = pl.BlockSpec(memory_space=pl.ANY)
    window = quarter // LANES
    members = 2 * nx
    dma = pltpu.SemaphoreType.DMA
    fields = jnp.transpose(atmosphere, (0, 1, 3, 2, 4))
    atm_out, ocean_out = pl.pallas_call(
        functools.partial(kernel, nx, nlat, 1.0 / (4 * nx)),
        out_shape=(
            jax.ShapeDtypeStruct(fields.shape, F32),
            jax.ShapeDtypeStruct((6, 2, 192), F32),
        ),
        in_specs=[hbm] * 7,
        out_specs=(vmem, vmem),
        scratch_shapes=[
            pltpu.VMEM((6, 2, 192), F32),
            pltpu.VMEM((6, 192), F32),
            pltpu.VMEM((6, lon), jnp.int32),
            pltpu.SMEM((2,), jnp.int32),
            pltpu.SMEM(parameter_table.shape[::-1], F32),
            pltpu.VMEM((8, 8), F32),
            pltpu.VMEM((6, 12, 2, 2, 8, lon), F32),
            pltpu.VMEM((2, 2, 8, 8, LANES), F32),
            pltpu.VMEM((2, 2, 8, LANES), F32),
            pltpu.VMEM((10, 2, 2, 8, lon), F32),
            pltpu.VMEM((2, 3, nx, 3, 8, 2 * LANES), F32),
            pltpu.VMEM((3, 8, lon), F32),
            pltpu.VMEM((2, 16, lon), F32),
            pltpu.VMEM((16, lon), F32),
            pltpu.VMEM((16, lon), F32),
            pltpu.VMEM((2, 16, lon), F32),
            pltpu.VMEM((2, lon // LANES + 2, 2, 8, LANES), F32),
            pltpu.VMEM((2, members - 1, window, 2, 8, LANES), F32),
            pltpu.VMEM((3, nx, window, 2, 8, LANES), F32),
            pltpu.VMEM((3, window, 2, 8, LANES), F32),
            pltpu.VMEM((3, 8, 2 * LANES), F32),
            dma((6,)),
            dma((2, 2, 3)),
            dma((2, 2, 3)),
            dma((2, 3, nx)),
            dma((2, 3, nx)),
            dma(()),
            dma(()),
            dma((2,)),
            dma((2,)),
            dma((2, members - 1)),
            dma((2, members - 1)),
            dma((3, nx)),
            dma((3, nx)),
            dma((2,)),
            dma((2,)),
            dma((6,)),
        ],
        compiler_params=pltpu.CompilerParams(
            collective_id=0, has_side_effects=True, vmem_limit_bytes=44 * 1024 * 1024
        ),
        name="coupled_window",
    )(
        *[
            pltpu.with_memory_space_constraint(operand, pltpu.HBM)
            for operand in (
                fields,
                jnp.transpose(ocean_state, (1, 0, 2)),
                viscosity,
                sea_mask,
                parameter_index,
                jnp.transpose(parameter_table),
                level_mix,
            )
        ]
    )
    atm_out, ocean_out = pl.pallas_call(
        store,
        out_shape=(jax.ShapeDtypeStruct(atm_out.shape, F32), jax.ShapeDtypeStruct(ocean_out.shape, F32)),
        in_specs=[anywhere] * 2,
        out_specs=(hbm, hbm),
        scratch_shapes=[dma((5,))],
        compiler_params=pltpu.CompilerParams(vmem_limit_bytes=1024 * 1024),
        name="store",
    )(atm_out, ocean_out)
    return jnp.transpose(atm_out, (0, 1, 3, 2, 4)), jnp.transpose(ocean_out, (1, 0, 2))


def solution(mesh):
    return jax.shard_map(
        functools.partial(body, mesh.shape["member"] // 2, mesh.shape["lat"]),
        mesh=mesh,
        in_specs=(
            P(None, "member", None, "lat", None),
            P(None, "lat", "member"),
            P("lat", "member"),
            P("lat", None),
            P("member"),
            P(),
            P(),
        ),
        out_specs=(P(None, "member", None, "lat", None), P(None, "lat", "member")),
        check_vma=False,
    )
```

```python
import functools

import jax
import jax.numpy as jnp
from jax import lax
from jax.experimental import pallas as pl
from jax.experimental.pallas import tpu as pltpu
from jax.sharding import PartitionSpec as P

ADVECTION = 0.1
OCEAN_GAIN = 0.5
OCEAN_DIFFUSION = 0.15
MESH = pl.DeviceIdType.MESH
F32 = jnp.float32
LANES = 128
CHUNK = 512


def tiles(vector, count):
    return jnp.concatenate([vector] * count, axis=1)


def sublane(shape):
    return lax.broadcasted_iota(jnp.int32, shape, 0)


def stack_rows(south, own, north):
    index = sublane(own.shape)
    middle = pltpu.roll(own, 5, 0)
    low = jnp.where(index < 5, pltpu.roll(south, 7, 0), middle)
    high = jnp.where(index < 3, middle, pltpu.roll(north, 3, 0))
    return jnp.concatenate([low, high], axis=0)


def join_chunks(even, odd):
    lane = lax.broadcasted_iota(jnp.int32, (8, LANES), 1)
    first = pltpu.roll(odd[:, :LANES], 64, 1)
    second = pltpu.roll(odd[:, LANES:], 64, 1)
    return jnp.concatenate(
        [even[:, :LANES], jnp.where(lane < 64, even[:, LANES:], first), jnp.where(lane < 64, first, second)], axis=1
    )


def kernel(
    nx, nlat, scale,
    atm, ocean_hbm, visc_hbm, mask_hbm, pick_hbm, table_hbm, mixing_hbm, atm_out, ocean_out,
    ocean_in, visc_in, mask_in, pick, table, mixing,
    state, coef, first, diff, surf, level, chunks, masks, ocean, visc, mask, force, part, gather_r, gather_f, seg,
    raw_ocean, raw_visc,
    load_sem, halo_send, halo_recv, seg_send, seg_recv, pair_send, pair_recv, mask_send, mask_recv,
    r_send, r_recv, f_send, f_recv, small_sem,
):
    me = lax.axis_index("member")
    lat = lax.axis_index("lat")
    x, yh = lax.rem(me, nx), lax.div(me, nx)
    has_south, has_north = lat > 0, lat < nlat - 1
    partner = ((1 - yh) * nx + x, lat)
    lon = mask_in.shape[1]
    pieces = lon // CHUNK
    quarter = lon // nx
    columns = lon // LANES
    window = quarter // LANES
    members = 2 * nx

    def peers():
        for side in (-1, 0, 1):
            for step in range(nx):
                if side or step:
                    yield side, step, (yh * nx + lax.rem(x + step, nx), lat + side)

    def guarded(side, run):
        if side < 0:
            pl.when(has_south)(run)
        elif side > 0:
            pl.when(has_north)(run)
        else:
            run()

    loads = [pltpu.make_async_copy(atm.at[:, :, r], state.at[0, r + 4], load_sem.at[r]) for r in range(6)]
    small = [
        pltpu.make_async_copy(source, target, small_sem.at[i])
        for i, (source, target) in enumerate(
            (
                (ocean_hbm, ocean_in), (visc_hbm, visc_in), (mask_hbm, mask_in),
                (pick_hbm, pick), (table_hbm, table), (mixing_hbm, mixing),
            )
        )
    ]
    for load in small:
        load.start()
    for load in loads:
        load.start()

    barrier = pltpu.get_barrier_semaphore()
    for step in range(1, members):
        device = (lax.rem(me + step, members), lat)
        pl.semaphore_signal(barrier, inc=1, device_id=device, device_id_type=MESH)
    for side, step, device in peers():
        if side:
            guarded(side, lambda device=device: pl.semaphore_signal(barrier, inc=1, device_id=device, device_id_type=MESH))

    pl.semaphore_wait(barrier, members - 1 + nx * has_south.astype(jnp.int32) + nx * has_north.astype(jnp.int32))

    def halo(cp, side, depth):
        row = 5 - depth if side > 0 else depth
        there = 3 - depth if side > 0 else 10 + depth
        source = atm.at[:, :, row] if cp == 0 else state.at[3, row + 4]
        k = (side + 1) // 2
        return pltpu.make_async_remote_copy(
            source, state.at[3 * cp, there], halo_send.at[cp, k, depth], halo_recv.at[cp, k, depth],
            device_id=(me, lat + side), device_id_type=MESH,
        )

    def start_halos(cp, depths):
        for depth in depths:
            for side in (-1, 1):
                guarded(side, lambda side=side, depth=depth: halo(cp, side, depth).start())

    def wait_halo(cp, depth):
        for side in (-1, 1):
            guarded(-side, lambda side=side: halo(cp, side, depth).wait_recv())

    def spread(stage, side, step, device):
        source = seg if stage == 0 else chunks.at[1 - yh, 1, x]
        target = chunks.at[yh if stage == 0 else 1 - yh, 1 - side, x]
        return pltpu.make_async_remote_copy(
            source, target, seg_send.at[stage, side + 1, step], seg_recv.at[stage, side + 1, step],
            device_id=device, device_id_type=MESH,
        )

    pairs = [
        pltpu.make_async_remote_copy(
            source, target, pair_send.at[k], pair_recv.at[k], device_id=partner, device_id_type=MESH
        )
        for k, (source, target) in enumerate(((ocean_hbm, raw_ocean), (visc_hbm, raw_visc)))
    ]

    def pack(ocean_ref, visc_ref):
        fields = []
        for field in range(3):
            lines = [visc_ref[r : r + 1, :] if field == 2 else ocean_ref[r, field : field + 1, :] for r in range(6)]
            block = jnp.concatenate(lines + [jnp.zeros((2, 192), F32)], axis=0)
            fields.append(jnp.concatenate([block, jnp.zeros((8, 64), F32)], axis=1))
        return jnp.stack(fields)

    def send_mask(side):
        return pltpu.make_async_remote_copy(
            masks.at[1], masks.at[1 - side], mask_send.at[(side + 1) // 2], mask_recv.at[(side + 1) // 2],
            device_id=(me, lat + side), device_id_type=MESH,
        )

    for pair in pairs:
        pair.start()
    start_halos(0, (0, 1))
    for load in small:
        load.wait()

    own = pack(ocean_in, visc_in)
    seg[...] = own
    chunks[yh, 1, x] = own
    for side, step, device in peers():
        guarded(side, lambda a=(side, step, device): spread(0, *a).start())
    masks[1] = jnp.zeros((8, lon), F32)
    masks[1, 0:6, :] = mask_in[...].astype(F32)
    row_zero = jnp.zeros((2, 2, 8, lon), F32)

    @pl.when(lat == 0)
    def _():
        for b in range(6):
            state[b, 3] = row_zero
        masks[0] = jnp.zeros((8, lon), F32)
        for i in range(nx):
            gather_f[0, i] = jnp.zeros((window, 2, 8, LANES), F32)
            for a in range(2):
                chunks[a, 0, i] = jnp.zeros((3, 8, 2 * LANES), F32)

    @pl.when(lat == nlat - 1)
    def _():
        for b in range(6):
            state[b, 10] = row_zero
        masks[2] = jnp.zeros((8, lon), F32)
        for i in range(nx):
            gather_f[2, i] = jnp.zeros((window, 2, 8, LANES), F32)
            for a in range(2):
                chunks[a, 2, i] = jnp.zeros((3, 8, 2 * LANES), F32)


    sub = sublane((8, LANES))
    top = sub == 0
    dif = [0.6 * table[0, pick[m]] for m in range(2)]
    exc = [[2.0 * table[1 + c, pick[m]] for m in range(2)] for c in range(2)]
    exv = [[jnp.where(top, exc[c][m], 0.0) for m in range(2)] for c in range(2)]
    mix = mixing[...]
    row8 = lax.broadcasted_iota(jnp.int32, (8, 8), 0)
    col8 = lax.broadcasted_iota(jnp.int32, (8, 8), 1)
    for m in range(2):
        diff[m, 0] = jnp.full((8, LANES), dif[m], F32)
        diff[m, 1] = jnp.full((8, LANES), 1.0 - 4.0 * dif[m], F32) / diff[m, 0]
        diff[m, 0] = (0.5 * ADVECTION) / diff[m, 0]
    level_zero = [[jnp.zeros((8, LANES), F32) for m in range(2)] for c in range(2)]
    for r in range(8):
        diagonal = jnp.sum(jnp.where(col8 == lax.rem(row8 - r + 8, 8), mix, 0.0), axis=1, keepdims=True)
        value = jnp.broadcast_to(diagonal, (8, LANES))
        if r == 0:
            value = value + 1.0
        for c in range(2):
            for m in range(2):
                weight = dif[m] * jnp.where(top, value * (1.0 - exc[c][m]), value)
                others = jnp.where(sub == r, 0.0, weight)
                level_zero[c][m] = level_zero[c][m] + (weight - others)
                coef[0, c, m, r] = pltpu.roll(weight, 4, 0) if r >= 4 else weight
                coef[1, c, m, r] = pltpu.roll(others, 4, 0) if r >= 4 else others
    for c in range(2):
        for m in range(2):
            first[c, m] = level_zero[c][m]

    def unit(source, target, e, m, k, kind):
        table_of = 1 if kind == 1 else 0
        width = CHUNK // LANES
        off, right, left = k * CHUNK, (k + 1) % pieces * CHUNK, (k * CHUNK - LANES) % lon
        gain = tiles(diff[m, 0], width)
        keep = tiles(diff[m, 1], width)
        wind = None
        for c in (1, 0):
            centre = state[source, e, c, m, :, off : off + CHUNK]
            ahead = state[source, e, c, m, :, right : right + LANES]
            behind = state[source, e, c, m, :, left : left + LANES]
            north = state[source, e + 1, c, m, :, off : off + CHUNK]
            south = state[source, e - 1, c, m, :, off : off + CHUNK]
            east = pltpu.roll(jnp.concatenate([centre, ahead], axis=1), CHUNK + LANES - 1, 1)[:, :CHUNK]
            west = pltpu.roll(jnp.concatenate([centre, behind], axis=1), 1, 1)[:, :CHUNK]
            if c == 1:
                wind = gain * centre
            advected = keep * centre + ((east + west) + (north + south)) - wind * (east - west)
            near = tiles(coef[table_of, c, m, 0], width) * advected
            far = tiles(coef[table_of, c, m, 4], width) * advected
            for r in range(1, 4):
                turned = pltpu.roll(advected, r, 0)
                near = near + tiles(coef[table_of, c, m, r], width) * turned
                far = far + tiles(coef[table_of, c, m, r + 4], width) * turned
            value = near + pltpu.roll(far, 4, 0)
            if kind == 2:
                value = value + surf[e - 3, c, m, :, off : off + CHUNK]
            if target == 6:
                atm_out[c, m, e - 4, :, off : off + CHUNK] = value
            else:
                state[target, e, c, m, :, off : off + CHUNK] = value

    def rows(source, target, start, stride, count, kind):
        def body(i, carry):
            row = start + i * stride
            inside = ((row >= 0) | has_south) & ((row <= 5) | has_north)

            @pl.when(inside)
            def _():
                for m in range(2):
                    for k in range(pieces):
                        unit(source, target, row + 4, m, k, kind)

            return carry

        lax.fori_loop(0, count, body, 0)

    def before_surface(cp, deep, between):
        b = 3 * cp
        for depth in range(deep):
            if between is not None and depth == 2:
                between()
            wait_halo(cp, depth)
            rows(b, b + 1, -depth, 5 + 2 * depth, 2, 0)
            if depth == 0:
                rows(b + 1, b + 2, 1, 1, 4, 1)
            else:
                rows(b + 1, b + 2, 1 - depth, 3 + 2 * depth, 2, 1)
        for row in range(1 - deep, 5 + deep):
            for c in range(2):
                for m in range(2):
                    level[c, m, row + 5 : row + 6, :] = state[b + 1, row + 4, c, m, 0:1, :]

    def add_surface(cp, deep):
        b = 3 * cp
        for m in range(2):
            keep, gain = tiles(diff[m, 1], columns), tiles(diff[m, 0], columns)
            keep, gain = jnp.concatenate([keep] * 2, axis=0), jnp.concatenate([gain] * 2, axis=0)
            wind = None
            for c in (1, 0):
                here = level[c, m] + exc[c][m] * ocean[c]
                if c == 1:
                    wind = gain * here
                east, west = pltpu.roll(here, lon - 1, 1), pltpu.roll(here, 1, 1)
                around = (east + west) + (pltpu.roll(here, 15, 0) + pltpu.roll(here, 1, 0))
                level[c, m] = keep * here + around - wind * (east - west)
        for row in range(2 - deep, 4 + deep):
            for c in range(2):
                line = jnp.broadcast_to(ocean[c, row + 5 : row + 6, :], (8, lon))
                for m in range(2):
                    value = tiles(exv[c][m], columns) * line
                    if 3 - deep <= row < 3 + deep:
                        surf[row + 1, c, m] = value

                    def run(value=value, c=c, m=m, row=row):
                        lowest = jnp.broadcast_to(level[c, m, row + 5 : row + 6, :], (8, lon))
                        change = tiles(first[c, m], columns) * lowest + value
                        state[b + 2, row + 4, c, m] = state[b + 2, row + 4, c, m] + change

                    guarded(-1 if row < 0 else 1 if row > 5 else 0, run)

    def advance(here, rate, sea, drive):
        width = here.shape[1]
        lap = (
            pltpu.roll(here, width - 1, 1) + pltpu.roll(here, 1, 1)
            + pltpu.roll(here, 15, 0) + pltpu.roll(here, 1, 0) - 4.0 * here
        )
        return here + sea * (OCEAN_GAIN * drive + rate * lap)

    def ocean_steps():
        for c in range(2):
            for q in range(nx):
                for j in range(window):
                    blocks = [gather_f[side, q, j, c] for side in range(3)]
                    start = q * quarter + j * LANES
                    force[c, :, start : start + LANES] = stack_rows(*blocks)
        for _ in range(2):
            for c in range(2):
                rate = visc[...] if c == 1 else OCEAN_DIFFUSION
                ocean[c] = advance(ocean[c], rate, mask[...], force[c])

    def first_tile(cp, member):
        if cp == 0:
            return window * lax.rem(member, nx)
        return lax.rem(lax.div(3 * member + 2 * columns - 1, 2), columns)

    def send_r(cp, step):
        to = lax.rem(me + step, members)
        return pltpu.make_async_remote_copy(
            part.at[cp, pl.ds(first_tile(cp, to), window)], gather_r.at[cp, step - 1],
            r_send.at[cp, step - 1], r_recv.at[cp, step - 1], device_id=(to, lat), device_id_type=MESH,
        )

    def send_f(side, step, device):
        return pltpu.make_async_remote_copy(
            gather_f.at[1, x], gather_f.at[1 - side, x], f_send.at[side + 1, step],
            f_recv.at[side + 1, step], device_id=device, device_id_type=MESH,
        )

    def flux(cp):
        for c in range(2):
            weights = [tiles(exv[c][m], columns) for m in range(2)]
            own = pltpu.roll(ocean[c], 11 + cp, 0)[0:8]
            value = jnp.zeros((8, lon), F32)
            for row in range(-cp, 6 + cp):
                if cp == 0:
                    last = [state[3, row + 4, c, m] for m in range(2)]
                elif 0 <= row < 6:
                    last = [atm_out[c, m, row] for m in range(2)]
                else:
                    last = [state[0, row + 4, c, m] for m in range(2)]
                line = weights[0] * last[0] + weights[1] * last[1]
                value = value + (pltpu.roll(line, row + cp, 0) if row + cp else line)
            value = value - (exc[c][0] + exc[c][1]) * own
            for j in range(columns + 2):
                start = j % columns * LANES
                part[cp, j, c] = value[:, start : start + LANES]
        for step in range(1, members):
            send_r(cp, step).start()

    def total(cp):
        for step in range(1, members):
            send_r(cp, step).wait_recv()
        parts = [part[cp, pl.ds(first_tile(cp, me), window)]] + [gather_r[cp, k] for k in range(members - 1)]
        while len(parts) > 1:
            parts = [a + b for a, b in zip(parts[0::2], parts[1::2])]
        return parts[0] * scale

    for load in loads:
        load.wait()
    rows(0, 1, 1, 1, 4, 0)
    for pair in pairs:
        pair.wait_recv()
    chunks[1 - yh, 1, x] = pack(raw_ocean, raw_visc)
    for side, step, device in peers():
        guarded(side, lambda a=(side, step, device): spread(1, *a).start())
    start_halos(0, (2,))
    for side in (-1, 1):
        guarded(side, lambda side=side: send_mask(side).start())
    before_surface(0, 3, None)
    for stage in range(2):
        for side, step, device in peers():
            guarded(-side, lambda a=(stage, side, step, device): spread(*a).wait_recv())
    for field in range(3):
        for q in range(nx):
            blocks = []
            for side in range(3):
                even = chunks[(2 * q) // nx, side, (2 * q) % nx, field]
                odd = chunks[(2 * q + 1) // nx, side, (2 * q + 1) % nx, field]
                blocks.append(join_chunks(even, odd))
            value = stack_rows(*blocks)
            span = slice(q * quarter, (q + 1) * quarter)
            if field == 2:
                visc[:, span] = value
            else:
                ocean[field, :, span] = value
    add_surface(0, 3)
    rows(2, 3, 0, 1, 6, 2)
    flux(0)
    start_halos(1, range(4))
    rows(3, 4, 1, 1, 4, 0)

    def broadcast():
        gather_f[1, x] = total(0)
        for side, step, device in peers():
            guarded(side, lambda a=(side, step, device): send_f(*a).start())

    before_surface(1, 4, broadcast)
    for side in (-1, 1):
        guarded(-side, lambda side=side: send_mask(side).wait_recv())
    mask[...] = stack_rows(masks[0], masks[1], masks[2])
    for side, step, device in peers():
        guarded(-side, lambda a=(side, step, device): send_f(*a).wait_recv())
    ocean_steps()

    add_surface(1, 4)
    rows(5, 0, -1, 7, 2, 2)
    rows(5, 6, 0, 1, 6, 2)
    flux(1)
    starts = [pl.multiple_of(lax.rem(first_tile(1, me) + j, columns) * LANES, LANES) for j in range(window)]

    def windowed(ref, *lead):
        return jnp.concatenate([ref[(*lead, slice(None), pl.ds(start, LANES))] for start in starts], axis=1)

    here = [windowed(ocean, c) for c in range(2)]
    rates = [OCEAN_DIFFUSION, windowed(visc)]
    sea = windowed(mask)
    odd = lax.rem(me, 2) == 1
    final = total(1)
    for c in range(2):
        drive = jnp.concatenate([jnp.concatenate([pltpu.roll(final[j, c], 4, 0)] * 2, axis=0) for j in range(window)], axis=1)
        value = advance(advance(here[c], rates[c], sea, drive), rates[c], sea, drive)
        value = jnp.where(odd, pltpu.roll(value, 64, 1), value)
        for r in range(6):
            ocean_out[r, c : c + 1, :] = value[r + 5 : r + 6, LANES : LANES + 192]

    for pair in pairs:
        pair.wait_send()
    for side in (-1, 1):
        guarded(side, lambda side=side: send_mask(side).wait_send())
        for cp in range(2):
            for depth in range(3 + cp):
                guarded(side, lambda a=(cp, side, depth): halo(*a).wait_send())
    for stage in range(2):
        for side, step, device in peers():
            guarded(side, lambda a=(stage, side, step, device): spread(*a).wait_send())
    for cp in range(2):
        for step in range(1, members):
            send_r(cp, step).wait_send()
    for side, step, device in peers():
        guarded(side, lambda a=(side, step, device): send_f(*a).wait_send())


def store(atm, ocean, atm_out, ocean_out, sem):
    copies = [pltpu.make_async_copy(ocean, ocean_out, sem.at[4])]
    copies += [pltpu.make_async_copy(atm.at[c, m], atm_out.at[c, m], sem.at[2 * c + m]) for c in range(2) for m in range(2)]
    for copy in copies:
        copy.start()
    for copy in copies:
        copy.wait()


def body(nx, nlat, atmosphere, ocean_state, viscosity, sea_mask, parameter_index, parameter_table, level_mix):
    lon = atmosphere.shape[4]
    quarter = lon // nx
    vmem = pl.BlockSpec(memory_space=pltpu.VMEM)
    hbm = pl.BlockSpec(memory_space=pltpu.HBM)
    anywhere = pl.BlockSpec(memory_space=pl.ANY)
    window = quarter // LANES
    members = 2 * nx
    dma = pltpu.SemaphoreType.DMA
    fields = jnp.transpose(atmosphere, (0, 1, 3, 2, 4))
    atm_out, ocean_out = pl.pallas_call(
        functools.partial(kernel, nx, nlat, 1.0 / (4 * nx)),
        out_shape=(
            jax.ShapeDtypeStruct(fields.shape, F32),
            jax.ShapeDtypeStruct((6, 2, 192), F32),
        ),
        in_specs=[hbm] * 7,
        out_specs=(vmem, vmem),
        scratch_shapes=[
            pltpu.VMEM((6, 2, 192), F32),
            pltpu.VMEM((6, 192), F32),
            pltpu.VMEM((6, lon), jnp.int32),
            pltpu.SMEM((2,), jnp.int32),
            pltpu.SMEM(parameter_table.shape[::-1], F32),
            pltpu.VMEM((8, 8), F32),
            pltpu.VMEM((6, 14, 2, 2, 8, lon), F32),
            pltpu.VMEM((2, 2, 2, 8, 8, LANES), F32),
            pltpu.VMEM((2, 2, 8, LANES), F32),
            pltpu.VMEM((2, 2, 8, LANES), F32),
            pltpu.VMEM((8, 2, 2, 8, lon), F32),
            pltpu.VMEM((2, 2, 16, lon), F32),
            pltpu.VMEM((2, 3, nx, 3, 8, 2 * LANES), F32),
            pltpu.VMEM((3, 8, lon), F32),
            pltpu.VMEM((2, 16, lon), F32),
            pltpu.VMEM((16, lon), F32),
            pltpu.VMEM((16, lon), F32),
            pltpu.VMEM((2, 16, lon), F32),
            pltpu.VMEM((2, lon // LANES + 2, 2, 8, LANES), F32),
            pltpu.VMEM((2, members - 1, window, 2, 8, LANES), F32),
            pltpu.VMEM((3, nx, window, 2, 8, LANES), F32),
            pltpu.VMEM((3, 8, 2 * LANES), F32),
            pltpu.VMEM((6, 2, 192), F32),
            pltpu.VMEM((6, 192), F32),
            dma((6,)),
            dma((2, 2, 4)),
            dma((2, 2, 4)),
            dma((2, 3, nx)),
            dma((2, 3, nx)),
            dma((2,)),
            dma((2,)),
            dma((2,)),
            dma((2,)),
            dma((2, members - 1)),
            dma((2, members - 1)),
            dma((3, nx)),
            dma((3, nx)),
            dma((6,)),
        ],
        compiler_params=pltpu.CompilerParams(
            collective_id=0, has_side_effects=True, vmem_limit_bytes=44 * 1024 * 1024
        ),
        name="coupled_window",
    )(
        *[
            pltpu.with_memory_space_constraint(operand, pltpu.HBM)
            for operand in (
                fields,
                jnp.transpose(ocean_state, (1, 0, 2)),
                viscosity,
                sea_mask,
                parameter_index,
                jnp.transpose(parameter_table),
                level_mix,
            )
        ]
    )
    atm_out, ocean_out = pl.pallas_call(
        store,
        out_shape=(jax.ShapeDtypeStruct(atm_out.shape, F32), jax.ShapeDtypeStruct(ocean_out.shape, F32)),
        in_specs=[anywhere] * 2,
        out_specs=(hbm, hbm),
        scratch_shapes=[dma((5,))],
        compiler_params=pltpu.CompilerParams(vmem_limit_bytes=1024 * 1024),
        name="store",
    )(atm_out, ocean_out)
    return jnp.transpose(atm_out, (0, 1, 3, 2, 4)), jnp.transpose(ocean_out, (1, 0, 2))


def solution(mesh):
    return jax.shard_map(
        functools.partial(body, mesh.shape["member"] // 2, mesh.shape["lat"]),
        mesh=mesh,
        in_specs=(
            P(None, "member", None, "lat", None),
            P(None, "lat", "member"),
            P("lat", "member"),
            P("lat", None),
            P("member"),
            P(),
            P(),
        ),
        out_specs=(P(None, "member", None, "lat", None), P(None, "lat", "member")),
        check_vma=False,
    )
```

```python
import functools

import jax
import jax.numpy as jnp
from jax import lax
from jax.experimental import pallas as pl
from jax.experimental.pallas import tpu as pltpu
from jax.sharding import PartitionSpec as P

ADVECTION = 0.1
OCEAN_GAIN = 0.5
OCEAN_DIFFUSION = 0.15
MESH = pl.DeviceIdType.MESH
F32 = jnp.float32
LANES = 128
CHUNK = 512


def tiles(vector, count):
    return jnp.concatenate([vector] * count, axis=1)


def sublane(shape):
    return lax.broadcasted_iota(jnp.int32, shape, 0)


def stack_rows(south, own, north):
    index = sublane(own.shape)
    middle = pltpu.roll(own, 5, 0)
    low = jnp.where(index < 5, pltpu.roll(south, 7, 0), middle)
    high = jnp.where(index < 3, middle, pltpu.roll(north, 3, 0))
    return jnp.concatenate([low, high], axis=0)


def join_chunks(even, odd):
    lane = lax.broadcasted_iota(jnp.int32, (8, LANES), 1)
    first = pltpu.roll(odd[:, :LANES], 64, 1)
    second = pltpu.roll(odd[:, LANES:], 64, 1)
    return jnp.concatenate(
        [even[:, :LANES], jnp.where(lane < 64, even[:, LANES:], first), jnp.where(lane < 64, first, second)], axis=1
    )


def kernel(
    nx, nlat, scale,
    atm, ocean_hbm, visc_hbm, mask_hbm, pick_hbm, table_hbm, mixing_hbm, atm_out, ocean_out,
    ocean_in, visc_in, mask_in, pick, table, mixing,
    state, coef, first, diff, surf, level, chunks, masks, ocean, visc, mask, force, part, gather_r, gather_f, seg,
    raw_ocean, raw_visc, bottom, tally,
    load_sem, halo_send, halo_recv, seg_send, seg_recv, pair_send, pair_recv, mask_send, mask_recv,
    r_send, r_recv, f_send, f_recv, small_sem,
):
    me = lax.axis_index("member")
    lat = lax.axis_index("lat")
    x, yh = lax.rem(me, nx), lax.div(me, nx)
    has_south, has_north = lat > 0, lat < nlat - 1
    partner = ((1 - yh) * nx + x, lat)
    lon = mask_in.shape[1]
    pieces = lon // CHUNK
    quarter = lon // nx
    columns = lon // LANES
    window = quarter // LANES
    members = 2 * nx

    def peers():
        for side in (-1, 0, 1):
            for step in range(nx):
                if side or step:
                    yield side, step, (yh * nx + lax.rem(x + step, nx), lat + side)

    def guarded(side, run):
        if side < 0:
            pl.when(has_south)(run)
        elif side > 0:
            pl.when(has_north)(run)
        else:
            run()

    loads = [pltpu.make_async_copy(atm.at[:, :, r], state.at[0, r + 4], load_sem.at[r]) for r in range(6)]
    small = [
        pltpu.make_async_copy(source, target, small_sem.at[i])
        for i, (source, target) in enumerate(
            (
                (ocean_hbm, ocean_in), (visc_hbm, visc_in), (mask_hbm, mask_in),
                (pick_hbm, pick), (table_hbm, table), (mixing_hbm, mixing),
            )
        )
    ]
    for load in small:
        load.start()
    for load in loads:
        load.start()

    barrier = pltpu.get_barrier_semaphore()
    for step in range(1, members):
        device = (lax.rem(me + step, members), lat)
        pl.semaphore_signal(barrier, inc=1, device_id=device, device_id_type=MESH)
    for side, step, device in peers():
        if side:
            guarded(side, lambda device=device: pl.semaphore_signal(barrier, inc=1, device_id=device, device_id_type=MESH))

    pl.semaphore_wait(barrier, members - 1 + nx * has_south.astype(jnp.int32) + nx * has_north.astype(jnp.int32))

    def halo(cp, side, depth):
        row = 5 - depth if side > 0 else depth
        there = 3 - depth if side > 0 else 10 + depth
        source = atm.at[:, :, row] if cp == 0 else state.at[3, row + 4]
        k = (side + 1) // 2
        return pltpu.make_async_remote_copy(
            source, state.at[3 * cp, there], halo_send.at[cp, k, depth], halo_recv.at[cp, k, depth],
            device_id=(me, lat + side), device_id_type=MESH,
        )

    def start_halos(cp, depths):
        for depth in depths:
            for side in (-1, 1):
                guarded(side, lambda side=side, depth=depth: halo(cp, side, depth).start())

    def wait_halo(cp, depth):
        for side in (-1, 1):
            guarded(-side, lambda side=side: halo(cp, side, depth).wait_recv())

    def spread(stage, side, step, device):
        source = seg if stage == 0 else chunks.at[1 - yh, 1, x]
        target = chunks.at[yh if stage == 0 else 1 - yh, 1 - side, x]
        return pltpu.make_async_remote_copy(
            source, target, seg_send.at[stage, side + 1, step], seg_recv.at[stage, side + 1, step],
            device_id=device, device_id_type=MESH,
        )

    pairs = [
        pltpu.make_async_remote_copy(
            source, target, pair_send.at[k], pair_recv.at[k], device_id=partner, device_id_type=MESH
        )
        for k, (source, target) in enumerate(((ocean_hbm, raw_ocean), (visc_hbm, raw_visc)))
    ]

    def pack(ocean_ref, visc_ref):
        fields = []
        for field in range(3):
            lines = [visc_ref[r : r + 1, :] if field == 2 else ocean_ref[r, field : field + 1, :] for r in range(6)]
            block = jnp.concatenate(lines + [jnp.zeros((2, 192), F32)], axis=0)
            fields.append(jnp.concatenate([block, jnp.zeros((8, 64), F32)], axis=1))
        return jnp.stack(fields)

    def send_mask(side):
        return pltpu.make_async_remote_copy(
            masks.at[1], masks.at[1 - side], mask_send.at[(side + 1) // 2], mask_recv.at[(side + 1) // 2],
            device_id=(me, lat + side), device_id_type=MESH,
        )

    for pair in pairs:
        pair.start()
    start_halos(0, (0, 1))
    for load in small:
        load.wait()

    own = pack(ocean_in, visc_in)
    seg[...] = own
    chunks[yh, 1, x] = own
    for side, step, device in peers():
        guarded(side, lambda a=(side, step, device): spread(0, *a).start())
    masks[1] = jnp.zeros((8, lon), F32)
    masks[1, 0:6, :] = mask_in[...].astype(F32)
    row_zero = jnp.zeros((2, 2, 8, lon), F32)

    @pl.when(lat == 0)
    def _():
        for b in range(6):
            state[b, 3] = row_zero
        masks[0] = jnp.zeros((8, lon), F32)
        for i in range(nx):
            gather_f[0, i] = jnp.zeros((window, 2, 8, LANES), F32)
            for a in range(2):
                chunks[a, 0, i] = jnp.zeros((3, 8, 2 * LANES), F32)

    @pl.when(lat == nlat - 1)
    def _():
        for b in range(6):
            state[b, 10] = row_zero
        masks[2] = jnp.zeros((8, lon), F32)
        for i in range(nx):
            gather_f[2, i] = jnp.zeros((window, 2, 8, LANES), F32)
            for a in range(2):
                chunks[a, 2, i] = jnp.zeros((3, 8, 2 * LANES), F32)


    sub = sublane((8, LANES))
    top = sub == 0
    dif = [0.6 * table[0, pick[m]] for m in range(2)]
    exc = [[2.0 * table[1 + c, pick[m]] for m in range(2)] for c in range(2)]
    exv = [[jnp.where(top, exc[c][m], 0.0) for m in range(2)] for c in range(2)]
    mix = mixing[...]
    row8 = lax.broadcasted_iota(jnp.int32, (8, 8), 0)
    col8 = lax.broadcasted_iota(jnp.int32, (8, 8), 1)
    for m in range(2):
        diff[m, 0] = jnp.full((8, LANES), dif[m], F32)
        diff[m, 1] = jnp.full((8, LANES), 1.0 - 4.0 * dif[m], F32) / diff[m, 0]
        diff[m, 0] = (0.5 * ADVECTION) / diff[m, 0]
    level_zero = [[jnp.zeros((8, LANES), F32) for m in range(2)] for c in range(2)]
    for r in range(8):
        diagonal = jnp.sum(jnp.where(col8 == lax.rem(row8 - r + 8, 8), mix, 0.0), axis=1, keepdims=True)
        value = jnp.broadcast_to(diagonal, (8, LANES))
        if r == 0:
            value = value + 1.0
        for c in range(2):
            for m in range(2):
                weight = dif[m] * jnp.where(top, value * (1.0 - exc[c][m]), value)
                others = jnp.where(sub == r, 0.0, weight)
                level_zero[c][m] = level_zero[c][m] + (weight - others)
                coef[0, c, m, r] = pltpu.roll(weight, 4, 0) if r >= 4 else weight
                coef[1, c, m, r] = pltpu.roll(others, 4, 0) if r >= 4 else others
    upper = jnp.sum(jnp.where(row8 == col8, jnp.broadcast_to(mix[0:1, :], (8, 8)), 0.0), axis=1, keepdims=True)
    upper = jnp.broadcast_to(upper, (8, LANES)) + jnp.where(top, 1.0, 0.0)
    share = [[exc[c][m] * (1.0 - exc[c][m]) for m in range(2)] for c in range(2)]
    for c in range(2):
        for m in range(2):
            first[c, m] = level_zero[c][m]
            bottom[c, m] = (share[c][m] * dif[m]) * upper

    def stencil(source, e, m, k):
        width = CHUNK // LANES
        off, right, left = k * CHUNK, (k + 1) % pieces * CHUNK, (k * CHUNK - LANES) % lon
        gain = tiles(diff[m, 0], width)
        keep = tiles(diff[m, 1], width)
        wind = None
        for c in (1, 0):
            centre = state[source, e, c, m, :, off : off + CHUNK]
            ahead = state[source, e, c, m, :, right : right + LANES]
            behind = state[source, e, c, m, :, left : left + LANES]
            north = state[source, e + 1, c, m, :, off : off + CHUNK]
            south = state[source, e - 1, c, m, :, off : off + CHUNK]
            east = pltpu.roll(jnp.concatenate([centre, ahead], axis=1), CHUNK + LANES - 1, 1)[:, :CHUNK]
            west = pltpu.roll(jnp.concatenate([centre, behind], axis=1), 1, 1)[:, :CHUNK]
            if c == 1:
                wind = gain * centre
            yield c, keep * centre + ((east + west) + (north + south)) - wind * (east - west)

    def mixed(advected, kind, c, m):
        width = CHUNK // LANES
        near = tiles(coef[kind, c, m, 0], width) * advected
        far = tiles(coef[kind, c, m, 4], width) * advected
        for r in range(1, 4):
            turned = pltpu.roll(advected, r, 0)
            near = near + tiles(coef[kind, c, m, r], width) * turned
            far = far + tiles(coef[kind, c, m, r + 4], width) * turned
        return near + pltpu.roll(far, 4, 0)

    def each_row(start, stride, count, run):
        def body(i, carry):
            row = start + i * stride
            inside = ((row >= 0) | has_south) & ((row <= 5) | has_north)
            pl.when(inside)(lambda: run(row))
            return carry

        lax.fori_loop(0, count, body, 0)

    def rows(source, target, start, stride, count, kind):
        def run(row):
            for m in range(2):
                for k in range(pieces):
                    for c, advected in stencil(source, row + 4, m, k):
                        state[target, row + 4, c, m, :, k * CHUNK : (k + 1) * CHUNK] = mixed(advected, kind, c, m)

        each_row(start, stride, count, run)

    def last_rows(source, target, start, count, shift):
        index = sublane((8, CHUNK))

        def run(row):
            for k in range(pieces):
                span = slice(k * CHUNK, (k + 1) * CHUNK)
                sums = [None, None]
                for m in range(2):
                    for c, advected in stencil(source, row + 4, m, k):
                        state[target, row + 4, c, m, :, span] = advected
                        term = tiles(bottom[c, m], CHUNK // LANES) * advected
                        sums[c] = term if sums[c] is None else sums[c] + term
                for c in range(2):
                    for turn in (4, 2, 1):
                        sums[c] = sums[c] + pltpu.roll(sums[c], turn, 0)
                    tally[c, :, span] = jnp.where(index == row + shift, sums[c], tally[c, :, span])

        for c in range(2):
            tally[c] = jnp.zeros((8, lon), F32)
        each_row(start, 1, count, run)

    def mix_rows(source, start, stride, count):
        def run(row):
            for m in range(2):
                for k in range(pieces):
                    span = slice(k * CHUNK, (k + 1) * CHUNK)
                    for c in range(2):
                        value = mixed(state[source, row + 4, c, m, :, span], 0, c, m) + surf[row + 1, c, m, :, span]
                        if source == 3:
                            state[3, row + 4, c, m, :, span] = value
                        else:
                            atm_out[c, m, row, :, span] = value

        each_row(start, stride, count, run)

    def before_surface(cp, deep, between):
        b = 3 * cp
        for depth in range(deep):
            if between is not None and depth == 2:
                between()
            wait_halo(cp, depth)
            rows(b, b + 1, -depth, 5 + 2 * depth, 2, 0)
            if depth == 0:
                rows(b + 1, b + 2, 1, 1, 4, 1)
            else:
                rows(b + 1, b + 2, 1 - depth, 3 + 2 * depth, 2, 1)
        for row in range(1 - deep, 5 + deep):
            for c in range(2):
                for m in range(2):
                    level[c, m, row + 5 : row + 6, :] = state[b + 1, row + 4, c, m, 0:1, :]

    def add_surface(cp, deep):
        b = 3 * cp
        for m in range(2):
            keep, gain = tiles(diff[m, 1], columns), tiles(diff[m, 0], columns)
            keep, gain = jnp.concatenate([keep] * 2, axis=0), jnp.concatenate([gain] * 2, axis=0)
            wind = None
            for c in (1, 0):
                here = level[c, m] + exc[c][m] * ocean[c]
                if c == 1:
                    wind = gain * here
                east, west = pltpu.roll(here, lon - 1, 1), pltpu.roll(here, 1, 1)
                around = (east + west) + (pltpu.roll(here, 15, 0) + pltpu.roll(here, 1, 0))
                level[c, m] = keep * here + around - wind * (east - west)
        for row in range(2 - deep, 4 + deep):
            for c in range(2):
                line = jnp.broadcast_to(ocean[c, row + 5 : row + 6, :], (8, lon))
                for m in range(2):
                    value = tiles(exv[c][m], columns) * line
                    if 3 - deep <= row < 3 + deep:
                        surf[row + 1, c, m] = value

                    def run(value=value, c=c, m=m, row=row):
                        lowest = jnp.broadcast_to(level[c, m, row + 5 : row + 6, :], (8, lon))
                        change = tiles(first[c, m], columns) * lowest + value
                        state[b + 2, row + 4, c, m] = state[b + 2, row + 4, c, m] + change

                    guarded(-1 if row < 0 else 1 if row > 5 else 0, run)

    def advance(here, rate, sea, drive):
        width = here.shape[1]
        lap = (
            pltpu.roll(here, width - 1, 1) + pltpu.roll(here, 1, 1)
            + pltpu.roll(here, 15, 0) + pltpu.roll(here, 1, 0) - 4.0 * here
        )
        return here + sea * (OCEAN_GAIN * drive + rate * lap)

    def ocean_steps():
        for c in range(2):
            for q in range(nx):
                for j in range(window):
                    blocks = [gather_f[side, q, j, c] for side in range(3)]
                    start = q * quarter + j * LANES
                    force[c, :, start : start + LANES] = stack_rows(*blocks)
        for _ in range(2):
            for c in range(2):
                rate = visc[...] if c == 1 else OCEAN_DIFFUSION
                ocean[c] = advance(ocean[c], rate, mask[...], force[c])

    def first_tile(cp, member):
        if cp == 0:
            return window * lax.rem(member, nx)
        return lax.rem(lax.div(3 * member + 2 * columns - 1, 2), columns)

    def send_r(cp, step):
        to = lax.rem(me + step, members)
        return pltpu.make_async_remote_copy(
            part.at[cp, pl.ds(first_tile(cp, to), window)], gather_r.at[cp, step - 1],
            r_send.at[cp, step - 1], r_recv.at[cp, step - 1], device_id=(to, lat), device_id_type=MESH,
        )

    def send_f(side, step, device):
        return pltpu.make_async_remote_copy(
            gather_f.at[1, x], gather_f.at[1 - side, x], f_send.at[side + 1, step],
            f_recv.at[side + 1, step], device_id=device, device_id_type=MESH,
        )

    def flux(cp):
        for c in range(2):
            own = pltpu.roll(ocean[c], 11 + cp, 0)[0:8]
            value = tally[c] - (share[c][0] + share[c][1]) * own
            for j in range(columns + 2):
                start = j % columns * LANES
                part[cp, j, c] = value[:, start : start + LANES]
        for step in range(1, members):
            send_r(cp, step).start()

    def total(cp):
        for step in range(1, members):
            send_r(cp, step).wait_recv()
        parts = [part[cp, pl.ds(first_tile(cp, me), window)]] + [gather_r[cp, k] for k in range(members - 1)]
        while len(parts) > 1:
            parts = [a + b for a, b in zip(parts[0::2], parts[1::2])]
        return parts[0] * scale

    for load in loads:
        load.wait()
    rows(0, 1, 1, 1, 4, 0)
    for pair in pairs:
        pair.wait_recv()
    chunks[1 - yh, 1, x] = pack(raw_ocean, raw_visc)
    for side, step, device in peers():
        guarded(side, lambda a=(side, step, device): spread(1, *a).start())
    start_halos(0, (2,))
    for side in (-1, 1):
        guarded(side, lambda side=side: send_mask(side).start())
    before_surface(0, 3, None)
    for stage in range(2):
        for side, step, device in peers():
            guarded(-side, lambda a=(stage, side, step, device): spread(*a).wait_recv())
    for field in range(3):
        for q in range(nx):
            blocks = []
            for side in range(3):
                even = chunks[(2 * q) // nx, side, (2 * q) % nx, field]
                odd = chunks[(2 * q + 1) // nx, side, (2 * q + 1) % nx, field]
                blocks.append(join_chunks(even, odd))
            value = stack_rows(*blocks)
            span = slice(q * quarter, (q + 1) * quarter)
            if field == 2:
                visc[:, span] = value
            else:
                ocean[field, :, span] = value
    add_surface(0, 3)
    last_rows(2, 3, 0, 6, 0)
    flux(0)
    mix_rows(3, 0, 5, 2)
    start_halos(1, (0,))
    mix_rows(3, 1, 3, 2)
    start_halos(1, (1,))
    mix_rows(3, 2, 1, 2)
    start_halos(1, (2, 3))
    rows(3, 4, 1, 1, 4, 0)

    def broadcast():
        gather_f[1, x] = total(0)
        for side, step, device in peers():
            guarded(side, lambda a=(side, step, device): send_f(*a).start())

    before_surface(1, 4, broadcast)
    for side in (-1, 1):
        guarded(-side, lambda side=side: send_mask(side).wait_recv())
    mask[...] = stack_rows(masks[0], masks[1], masks[2])
    for side, step, device in peers():
        guarded(-side, lambda a=(side, step, device): send_f(*a).wait_recv())
    ocean_steps()

    add_surface(1, 4)
    last_rows(5, 0, -1, 8, 1)
    flux(1)
    mix_rows(0, 0, 1, 6)
    starts = [pl.multiple_of(lax.rem(first_tile(1, me) + j, columns) * LANES, LANES) for j in range(window)]

    def windowed(ref, *lead):
        return jnp.concatenate([ref[(*lead, slice(None), pl.ds(start, LANES))] for start in starts], axis=1)

    here = [windowed(ocean, c) for c in range(2)]
    rates = [OCEAN_DIFFUSION, windowed(visc)]
    sea = windowed(mask)
    odd = lax.rem(me, 2) == 1
    final = total(1)
    for c in range(2):
        drive = jnp.concatenate([jnp.concatenate([pltpu.roll(final[j, c], 4, 0)] * 2, axis=0) for j in range(window)], axis=1)
        value = advance(advance(here[c], rates[c], sea, drive), rates[c], sea, drive)
        value = jnp.where(odd, pltpu.roll(value, 64, 1), value)
        for r in range(6):
            ocean_out[r, c : c + 1, :] = value[r + 5 : r + 6, LANES : LANES + 192]

    for pair in pairs:
        pair.wait_send()
    for side in (-1, 1):
        guarded(side, lambda side=side: send_mask(side).wait_send())
        for cp in range(2):
            for depth in range(3 + cp):
                guarded(side, lambda a=(cp, side, depth): halo(*a).wait_send())
    for stage in range(2):
        for side, step, device in peers():
            guarded(side, lambda a=(stage, side, step, device): spread(*a).wait_send())
    for cp in range(2):
        for step in range(1, members):
            send_r(cp, step).wait_send()
    for side, step, device in peers():
        guarded(side, lambda a=(side, step, device): send_f(*a).wait_send())


def store(atm, ocean, atm_out, ocean_out, sem):
    copies = [pltpu.make_async_copy(ocean, ocean_out, sem.at[4])]
    copies += [pltpu.make_async_copy(atm.at[c, m], atm_out.at[c, m], sem.at[2 * c + m]) for c in range(2) for m in range(2)]
    for copy in copies:
        copy.start()
    for copy in copies:
        copy.wait()


def body(nx, nlat, atmosphere, ocean_state, viscosity, sea_mask, parameter_index, parameter_table, level_mix):
    lon = atmosphere.shape[4]
    quarter = lon // nx
    vmem = pl.BlockSpec(memory_space=pltpu.VMEM)
    hbm = pl.BlockSpec(memory_space=pltpu.HBM)
    anywhere = pl.BlockSpec(memory_space=pl.ANY)
    window = quarter // LANES
    members = 2 * nx
    dma = pltpu.SemaphoreType.DMA
    fields = jnp.transpose(atmosphere, (0, 1, 3, 2, 4))
    atm_out, ocean_out = pl.pallas_call(
        functools.partial(kernel, nx, nlat, 1.0 / (4 * nx)),
        out_shape=(
            jax.ShapeDtypeStruct(fields.shape, F32),
            jax.ShapeDtypeStruct((6, 2, 192), F32),
        ),
        in_specs=[hbm] * 7,
        out_specs=(vmem, vmem),
        scratch_shapes=[
            pltpu.VMEM((6, 2, 192), F32),
            pltpu.VMEM((6, 192), F32),
            pltpu.VMEM((6, lon), jnp.int32),
            pltpu.SMEM((2,), jnp.int32),
            pltpu.SMEM(parameter_table.shape[::-1], F32),
            pltpu.VMEM((8, 8), F32),
            pltpu.VMEM((6, 14, 2, 2, 8, lon), F32),
            pltpu.VMEM((2, 2, 2, 8, 8, LANES), F32),
            pltpu.VMEM((2, 2, 8, LANES), F32),
            pltpu.VMEM((2, 2, 8, LANES), F32),
            pltpu.VMEM((8, 2, 2, 8, lon), F32),
            pltpu.VMEM((2, 2, 16, lon), F32),
            pltpu.VMEM((2, 3, nx, 3, 8, 2 * LANES), F32),
            pltpu.VMEM((3, 8, lon), F32),
            pltpu.VMEM((2, 16, lon), F32),
            pltpu.VMEM((16, lon), F32),
            pltpu.VMEM((16, lon), F32),
            pltpu.VMEM((2, 16, lon), F32),
            pltpu.VMEM((2, lon // LANES + 2, 2, 8, LANES), F32),
            pltpu.VMEM((2, members - 1, window, 2, 8, LANES), F32),
            pltpu.VMEM((3, nx, window, 2, 8, LANES), F32),
            pltpu.VMEM((3, 8, 2 * LANES), F32),
            pltpu.VMEM((6, 2, 192), F32),
            pltpu.VMEM((6, 192), F32),
            pltpu.VMEM((2, 2, 8, LANES), F32),
            pltpu.VMEM((2, 8, lon), F32),
            dma((6,)),
            dma((2, 2, 4)),
            dma((2, 2, 4)),
            dma((2, 3, nx)),
            dma((2, 3, nx)),
            dma((2,)),
            dma((2,)),
            dma((2,)),
            dma((2,)),
            dma((2, members - 1)),
            dma((2, members - 1)),
            dma((3, nx)),
            dma((3, nx)),
            dma((6,)),
        ],
        compiler_params=pltpu.CompilerParams(
            collective_id=0, has_side_effects=True, vmem_limit_bytes=44 * 1024 * 1024
        ),
        name="coupled_window",
    )(
        *[
            pltpu.with_memory_space_constraint(operand, pltpu.HBM)
            for operand in (
                fields,
                jnp.transpose(ocean_state, (1, 0, 2)),
                viscosity,
                sea_mask,
                parameter_index,
                jnp.transpose(parameter_table),
                level_mix,
            )
        ]
    )
    atm_out, ocean_out = pl.pallas_call(
        store,
        out_shape=(jax.ShapeDtypeStruct(atm_out.shape, F32), jax.ShapeDtypeStruct(ocean_out.shape, F32)),
        in_specs=[anywhere] * 2,
        out_specs=(hbm, hbm),
        scratch_shapes=[dma((5,))],
        compiler_params=pltpu.CompilerParams(vmem_limit_bytes=1024 * 1024),
        name="store",
    )(atm_out, ocean_out)
    return jnp.transpose(atm_out, (0, 1, 3, 2, 4)), jnp.transpose(ocean_out, (1, 0, 2))


def solution(mesh):
    return jax.shard_map(
        functools.partial(body, mesh.shape["member"] // 2, mesh.shape["lat"]),
        mesh=mesh,
        in_specs=(
            P(None, "member", None, "lat", None),
            P(None, "lat", "member"),
            P("lat", "member"),
            P("lat", None),
            P("member"),
            P(),
            P(),
        ),
        out_specs=(P(None, "member", None, "lat", None), P(None, "lat", "member")),
        check_vma=False,
    )
```

```python
import functools

import jax
import jax.numpy as jnp
from jax import lax
from jax.experimental import pallas as pl
from jax.experimental.pallas import tpu as pltpu
from jax.sharding import PartitionSpec as P

ADVECTION = 0.1
OCEAN_GAIN = 0.5
OCEAN_DIFFUSION = 0.15
MESH = pl.DeviceIdType.MESH
F32 = jnp.float32
LANES = 128
CHUNK = 512


def tiles(vector, count):
    return jnp.concatenate([vector] * count, axis=1)


def sublane(shape):
    return lax.broadcasted_iota(jnp.int32, shape, 0)


def stack_rows(south, own, north):
    index = sublane(own.shape)
    middle = pltpu.roll(own, 5, 0)
    low = jnp.where(index < 5, pltpu.roll(south, 7, 0), middle)
    high = jnp.where(index < 3, middle, pltpu.roll(north, 3, 0))
    return jnp.concatenate([low, high], axis=0)


def join_chunks(even, odd):
    lane = lax.broadcasted_iota(jnp.int32, (8, LANES), 1)
    first = pltpu.roll(odd[:, :LANES], 64, 1)
    second = pltpu.roll(odd[:, LANES:], 64, 1)
    return jnp.concatenate(
        [even[:, :LANES], jnp.where(lane < 64, even[:, LANES:], first), jnp.where(lane < 64, first, second)], axis=1
    )


def kernel(
    nx, nlat, scale,
    atm, ocean_hbm, visc_hbm, mask_hbm, pick_hbm, table_hbm, mixing_hbm, atm_out, ocean_out,
    ocean_in, visc_in, mask_in, pick, table, mixing,
    state, coef, first, diff, surf, level, chunks, masks, ocean, visc, mask, force, part, gather_r, gather_f, seg,
    raw_ocean, raw_visc, bottom, tally,
    load_sem, halo_send, halo_recv, seg_send, seg_recv, pair_send, pair_recv, mask_send, mask_recv,
    r_send, r_recv, f_send, f_recv, small_sem,
):
    me = lax.axis_index("member")
    lat = lax.axis_index("lat")
    x, yh = lax.rem(me, nx), lax.div(me, nx)
    has_south, has_north = lat > 0, lat < nlat - 1
    partner = ((1 - yh) * nx + x, lat)
    lon = mask_in.shape[1]
    pieces = lon // CHUNK
    quarter = lon // nx
    columns = lon // LANES
    window = quarter // LANES
    members = 2 * nx

    def peers():
        for side in (-1, 1, 0):
            for step in (2, 1, 3, 0):
                if side or step:
                    yield side, step, (yh * nx + lax.rem(x + step, nx), lat + side)

    def guarded(side, run):
        if side < 0:
            pl.when(has_south)(run)
        elif side > 0:
            pl.when(has_north)(run)
        else:
            run()

    loads = [pltpu.make_async_copy(atm.at[:, :, r], state.at[0, r + 4], load_sem.at[r]) for r in range(6)]
    small = [
        pltpu.make_async_copy(source, target, small_sem.at[i])
        for i, (source, target) in enumerate(
            (
                (ocean_hbm, ocean_in), (visc_hbm, visc_in), (mask_hbm, mask_in),
                (pick_hbm, pick), (table_hbm, table), (mixing_hbm, mixing),
            )
        )
    ]
    for load in small:
        load.start()
    for load in loads:
        load.start()

    barrier = pltpu.get_barrier_semaphore()
    for step in range(1, members):
        device = (lax.rem(me + step, members), lat)
        pl.semaphore_signal(barrier, inc=1, device_id=device, device_id_type=MESH)
    for side, step, device in peers():
        if side:
            guarded(side, lambda device=device: pl.semaphore_signal(barrier, inc=1, device_id=device, device_id_type=MESH))

    pl.semaphore_wait(barrier, members - 1 + nx * has_south.astype(jnp.int32) + nx * has_north.astype(jnp.int32))

    def halo(cp, side, depth):
        row = 5 - depth if side > 0 else depth
        there = 3 - depth if side > 0 else 10 + depth
        source = atm.at[:, :, row] if cp == 0 else state.at[3, row + 4]
        k = (side + 1) // 2
        return pltpu.make_async_remote_copy(
            source, state.at[3 * cp, there], halo_send.at[cp, k, depth], halo_recv.at[cp, k, depth],
            device_id=(me, lat + side), device_id_type=MESH,
        )

    def start_halos(cp, depths):
        for depth in depths:
            for side in (-1, 1):
                guarded(side, lambda side=side, depth=depth: halo(cp, side, depth).start())

    def wait_halo(cp, depth):
        for side in (-1, 1):
            guarded(-side, lambda side=side: halo(cp, side, depth).wait_recv())

    def spread(stage, side, step, device):
        source = seg if stage == 0 else chunks.at[1 - yh, 1, x]
        target = chunks.at[yh if stage == 0 else 1 - yh, 1 - side, x]
        return pltpu.make_async_remote_copy(
            source, target, seg_send.at[stage, side + 1, step], seg_recv.at[stage, side + 1, step],
            device_id=device, device_id_type=MESH,
        )

    pairs = [
        pltpu.make_async_remote_copy(
            source, target, pair_send.at[k], pair_recv.at[k], device_id=partner, device_id_type=MESH
        )
        for k, (source, target) in enumerate(((ocean_hbm, raw_ocean), (visc_hbm, raw_visc)))
    ]

    def pack(ocean_ref, visc_ref):
        fields = []
        for field in range(3):
            lines = [visc_ref[r : r + 1, :] if field == 2 else ocean_ref[r, field : field + 1, :] for r in range(6)]
            block = jnp.concatenate(lines + [jnp.zeros((2, 192), F32)], axis=0)
            fields.append(jnp.concatenate([block, jnp.zeros((8, 64), F32)], axis=1))
        return jnp.stack(fields)

    def send_mask(side):
        return pltpu.make_async_remote_copy(
            masks.at[1], masks.at[1 - side], mask_send.at[(side + 1) // 2], mask_recv.at[(side + 1) // 2],
            device_id=(me, lat + side), device_id_type=MESH,
        )

    for pair in pairs:
        pair.start()
    start_halos(0, (0, 1, 2))
    for load in small:
        load.wait()

    own = pack(ocean_in, visc_in)
    seg[...] = own
    chunks[yh, 1, x] = own
    for side, step, device in peers():
        guarded(side, lambda a=(side, step, device): spread(0, *a).start())
    masks[1] = jnp.zeros((8, lon), F32)
    masks[1, 0:6, :] = mask_in[...].astype(F32)
    row_zero = jnp.zeros((2, 2, 8, lon), F32)

    @pl.when(lat == 0)
    def _():
        for b in range(6):
            state[b, 3] = row_zero
        masks[0] = jnp.zeros((8, lon), F32)
        for i in range(nx):
            gather_f[0, i] = jnp.zeros((window, 2, 8, LANES), F32)
            for a in range(2):
                chunks[a, 0, i] = jnp.zeros((3, 8, 2 * LANES), F32)

    @pl.when(lat == nlat - 1)
    def _():
        for b in range(6):
            state[b, 10] = row_zero
        masks[2] = jnp.zeros((8, lon), F32)
        for i in range(nx):
            gather_f[2, i] = jnp.zeros((window, 2, 8, LANES), F32)
            for a in range(2):
                chunks[a, 2, i] = jnp.zeros((3, 8, 2 * LANES), F32)


    sub = sublane((8, LANES))
    top = sub == 0
    dif = [0.6 * table[0, pick[m]] for m in range(2)]
    exc = [[2.0 * table[1 + c, pick[m]] for m in range(2)] for c in range(2)]
    exv = [[jnp.where(top, exc[c][m], 0.0) for m in range(2)] for c in range(2)]
    mix = mixing[...]
    row8 = lax.broadcasted_iota(jnp.int32, (8, 8), 0)
    col8 = lax.broadcasted_iota(jnp.int32, (8, 8), 1)
    for m in range(2):
        diff[m, 0] = jnp.full((8, LANES), dif[m], F32)
        diff[m, 1] = jnp.full((8, LANES), 1.0 - 4.0 * dif[m], F32) / diff[m, 0]
        diff[m, 0] = (0.5 * ADVECTION) / diff[m, 0]
    level_zero = [[jnp.zeros((8, LANES), F32) for m in range(2)] for c in range(2)]
    for r in range(8):
        diagonal = jnp.sum(jnp.where(col8 == lax.rem(row8 - r + 8, 8), mix, 0.0), axis=1, keepdims=True)
        value = jnp.broadcast_to(diagonal, (8, LANES))
        if r == 0:
            value = value + 1.0
        for c in range(2):
            for m in range(2):
                weight = dif[m] * jnp.where(top, value * (1.0 - exc[c][m]), value)
                others = jnp.where(sub == r, 0.0, weight)
                level_zero[c][m] = level_zero[c][m] + (weight - others)
                coef[0, c, m, r] = pltpu.roll(weight, 4, 0) if r >= 4 else weight
                coef[1, c, m, r] = pltpu.roll(others, 4, 0) if r >= 4 else others
    upper = jnp.sum(jnp.where(row8 == col8, jnp.broadcast_to(mix[0:1, :], (8, 8)), 0.0), axis=1, keepdims=True)
    upper = jnp.broadcast_to(upper, (8, LANES)) + jnp.where(top, 1.0, 0.0)
    share = [[exc[c][m] * (1.0 - exc[c][m]) for m in range(2)] for c in range(2)]
    for c in range(2):
        for m in range(2):
            first[c, m] = level_zero[c][m]
            bottom[c, m] = (share[c][m] * dif[m]) * upper

    def stencil(source, e, m, k):
        width = CHUNK // LANES
        off, right, left = k * CHUNK, (k + 1) % pieces * CHUNK, (k * CHUNK - LANES) % lon
        gain = tiles(diff[m, 0], width)
        keep = tiles(diff[m, 1], width)
        wind = None
        for c in (1, 0):
            centre = state[source, e, c, m, :, off : off + CHUNK]
            ahead = state[source, e, c, m, :, right : right + LANES]
            behind = state[source, e, c, m, :, left : left + LANES]
            north = state[source, e + 1, c, m, :, off : off + CHUNK]
            south = state[source, e - 1, c, m, :, off : off + CHUNK]
            east = pltpu.roll(jnp.concatenate([centre, ahead], axis=1), CHUNK + LANES - 1, 1)[:, :CHUNK]
            west = pltpu.roll(jnp.concatenate([centre, behind], axis=1), 1, 1)[:, :CHUNK]
            if c == 1:
                wind = gain * centre
            yield c, keep * centre + ((east + west) + (north + south)) - wind * (east - west)

    def mixed(advected, kind, c, m):
        width = CHUNK // LANES
        near = tiles(coef[kind, c, m, 0], width) * advected
        far = tiles(coef[kind, c, m, 4], width) * advected
        for r in range(1, 4):
            turned = pltpu.roll(advected, r, 0)
            near = near + tiles(coef[kind, c, m, r], width) * turned
            far = far + tiles(coef[kind, c, m, r + 4], width) * turned
        return near + pltpu.roll(far, 4, 0)

    def each_row(start, stride, count, run):
        def body(i, carry):
            row = start + i * stride
            inside = ((row >= 0) | has_south) & ((row <= 5) | has_north)
            pl.when(inside)(lambda: run(row))
            return carry

        lax.fori_loop(0, count, body, 0)

    def rows(source, target, start, stride, count, kind):
        def run(row):
            for m in range(2):
                for k in range(pieces):
                    for c, advected in stencil(source, row + 4, m, k):
                        state[target, row + 4, c, m, :, k * CHUNK : (k + 1) * CHUNK] = mixed(advected, kind, c, m)

        each_row(start, stride, count, run)

    def last_rows(source, target, start, count, shift):
        index = sublane((8, CHUNK))

        def run(row):
            for k in range(pieces):
                span = slice(k * CHUNK, (k + 1) * CHUNK)
                sums = [None, None]
                for m in range(2):
                    for c, advected in stencil(source, row + 4, m, k):
                        state[target, row + 4, c, m, :, span] = advected
                        term = tiles(bottom[c, m], CHUNK // LANES) * advected
                        sums[c] = term if sums[c] is None else sums[c] + term
                for c in range(2):
                    for turn in (4, 2, 1):
                        sums[c] = sums[c] + pltpu.roll(sums[c], turn, 0)
                    tally[c, :, span] = jnp.where(index == row + shift, sums[c], tally[c, :, span])

        for c in range(2):
            tally[c] = jnp.zeros((8, lon), F32)
        each_row(start, 1, count, run)

    def mix_rows(source, start, stride, count):
        def run(row):
            for m in range(2):
                for k in range(pieces):
                    span = slice(k * CHUNK, (k + 1) * CHUNK)
                    for c in range(2):
                        value = mixed(state[source, row + 4, c, m, :, span], 0, c, m) + surf[row + 1, c, m, :, span]
                        if source == 3:
                            state[3, row + 4, c, m, :, span] = value
                        else:
                            atm_out[c, m, row, :, span] = value

        each_row(start, stride, count, run)

    def before_surface(cp, deep, between):
        b = 3 * cp
        for depth in range(deep):
            if between is not None and depth == 0:
                between()
            wait_halo(cp, depth)
            rows(b, b + 1, -depth, 5 + 2 * depth, 2, 0)
            if depth == 0:
                rows(b + 1, b + 2, 1, 1, 4, 1)
            else:
                rows(b + 1, b + 2, 1 - depth, 3 + 2 * depth, 2, 1)
        for row in range(1 - deep, 5 + deep):
            for c in range(2):
                for m in range(2):
                    level[c, m, row + 5 : row + 6, :] = state[b + 1, row + 4, c, m, 0:1, :]

    def add_surface(cp, deep):
        b = 3 * cp
        for m in range(2):
            keep, gain = tiles(diff[m, 1], columns), tiles(diff[m, 0], columns)
            keep, gain = jnp.concatenate([keep] * 2, axis=0), jnp.concatenate([gain] * 2, axis=0)
            wind = None
            for c in (1, 0):
                here = level[c, m] + exc[c][m] * ocean[c]
                if c == 1:
                    wind = gain * here
                east, west = pltpu.roll(here, lon - 1, 1), pltpu.roll(here, 1, 1)
                around = (east + west) + (pltpu.roll(here, 15, 0) + pltpu.roll(here, 1, 0))
                level[c, m] = keep * here + around - wind * (east - west)
        for row in range(2 - deep, 4 + deep):
            for c in range(2):
                line = jnp.broadcast_to(ocean[c, row + 5 : row + 6, :], (8, lon))
                for m in range(2):
                    value = tiles(exv[c][m], columns) * line
                    if 3 - deep <= row < 3 + deep:
                        surf[row + 1, c, m] = value

                    def run(value=value, c=c, m=m, row=row):
                        lowest = jnp.broadcast_to(level[c, m, row + 5 : row + 6, :], (8, lon))
                        change = tiles(first[c, m], columns) * lowest + value
                        state[b + 2, row + 4, c, m] = state[b + 2, row + 4, c, m] + change

                    guarded(-1 if row < 0 else 1 if row > 5 else 0, run)

    def advance(here, rate, sea, drive):
        width = here.shape[1]
        lap = (
            pltpu.roll(here, width - 1, 1) + pltpu.roll(here, 1, 1)
            + pltpu.roll(here, 15, 0) + pltpu.roll(here, 1, 0) - 4.0 * here
        )
        return here + sea * (OCEAN_GAIN * drive + rate * lap)

    def ocean_steps():
        for c in range(2):
            for q in range(nx):
                for j in range(window):
                    blocks = [gather_f[side, q, j, c] for side in range(3)]
                    start = q * quarter + j * LANES
                    force[c, :, start : start + LANES] = stack_rows(*blocks)
        for _ in range(2):
            for c in range(2):
                rate = visc[...] if c == 1 else OCEAN_DIFFUSION
                ocean[c] = advance(ocean[c], rate, mask[...], force[c])

    def first_tile(cp, member):
        if cp == 0:
            return window * lax.rem(member, nx)
        return lax.rem(lax.div(3 * member + 2 * columns - 1, 2), columns)

    def send_r(cp, step):
        to = lax.rem(me + step, members)
        return pltpu.make_async_remote_copy(
            part.at[cp, pl.ds(first_tile(cp, to), window)], gather_r.at[cp, step - 1],
            r_send.at[cp, step - 1], r_recv.at[cp, step - 1], device_id=(to, lat), device_id_type=MESH,
        )

    def send_f(side, step, device):
        return pltpu.make_async_remote_copy(
            gather_f.at[1, x], gather_f.at[1 - side, x], f_send.at[side + 1, step],
            f_recv.at[side + 1, step], device_id=device, device_id_type=MESH,
        )

    def flux(cp):
        for c in range(2):
            own = pltpu.roll(ocean[c], 11 + cp, 0)[0:8]
            value = tally[c] - (share[c][0] + share[c][1]) * own
            for j in range(columns + 2):
                start = j % columns * LANES
                part[cp, j, c] = value[:, start : start + LANES]
        for step in (2, 6, 3, 5, 4, 1, 7):
            send_r(cp, step).start()

    def total(cp):
        for step in range(1, members):
            send_r(cp, step).wait_recv()
        parts = [part[cp, pl.ds(first_tile(cp, me), window)]] + [gather_r[cp, k] for k in range(members - 1)]
        while len(parts) > 1:
            parts = [a + b for a, b in zip(parts[0::2], parts[1::2])]
        return parts[0] * scale

    for load in loads:
        load.wait()
    rows(0, 1, 1, 1, 4, 0)
    for pair in pairs:
        pair.wait_recv()
    chunks[1 - yh, 1, x] = pack(raw_ocean, raw_visc)
    for side, step, device in peers():
        guarded(side, lambda a=(side, step, device): spread(1, *a).start())
    for side in (-1, 1):
        guarded(side, lambda side=side: send_mask(side).start())
    before_surface(0, 3, None)
    for stage in range(2):
        for side, step, device in peers():
            guarded(-side, lambda a=(stage, side, step, device): spread(*a).wait_recv())
    for field in range(3):
        for q in range(nx):
            blocks = []
            for side in range(3):
                even = chunks[(2 * q) // nx, side, (2 * q) % nx, field]
                odd = chunks[(2 * q + 1) // nx, side, (2 * q + 1) % nx, field]
                blocks.append(join_chunks(even, odd))
            value = stack_rows(*blocks)
            span = slice(q * quarter, (q + 1) * quarter)
            if field == 2:
                visc[:, span] = value
            else:
                ocean[field, :, span] = value
    add_surface(0, 3)
    last_rows(2, 3, 0, 6, 0)
    flux(0)
    mix_rows(3, 0, 5, 2)
    start_halos(1, (0,))
    mix_rows(3, 1, 3, 2)
    start_halos(1, (1,))
    mix_rows(3, 2, 1, 2)
    start_halos(1, (2, 3))
    rows(3, 4, 1, 1, 4, 0)

    def broadcast():
        gather_f[1, x] = total(0)
        for side, step, device in peers():
            guarded(side, lambda a=(side, step, device): send_f(*a).start())

    before_surface(1, 4, broadcast)
    for side in (-1, 1):
        guarded(-side, lambda side=side: send_mask(side).wait_recv())
    mask[...] = stack_rows(masks[0], masks[1], masks[2])
    for side, step, device in peers():
        guarded(-side, lambda a=(side, step, device): send_f(*a).wait_recv())
    ocean_steps()

    add_surface(1, 4)
    last_rows(5, 0, -1, 8, 1)
    flux(1)
    mix_rows(0, 0, 1, 6)
    starts = [pl.multiple_of(lax.rem(first_tile(1, me) + j, columns) * LANES, LANES) for j in range(window)]

    def windowed(ref, *lead):
        return jnp.concatenate([ref[(*lead, slice(None), pl.ds(start, LANES))] for start in starts], axis=1)

    here = [windowed(ocean, c) for c in range(2)]
    rates = [OCEAN_DIFFUSION, windowed(visc)]
    sea = windowed(mask)
    odd = lax.rem(me, 2) == 1
    final = total(1)
    for c in range(2):
        drive = jnp.concatenate([jnp.concatenate([pltpu.roll(final[j, c], 4, 0)] * 2, axis=0) for j in range(window)], axis=1)
        value = advance(advance(here[c], rates[c], sea, drive), rates[c], sea, drive)
        value = jnp.where(odd, pltpu.roll(value, 64, 1), value)
        for r in range(6):
            ocean_out[r, c : c + 1, :] = value[r + 5 : r + 6, LANES : LANES + 192]

    for pair in pairs:
        pair.wait_send()
    for side in (-1, 1):
        guarded(side, lambda side=side: send_mask(side).wait_send())
        for cp in range(2):
            for depth in range(3 + cp):
                guarded(side, lambda a=(cp, side, depth): halo(*a).wait_send())
    for stage in range(2):
        for side, step, device in peers():
            guarded(side, lambda a=(stage, side, step, device): spread(*a).wait_send())
    for cp in range(2):
        for step in range(1, members):
            send_r(cp, step).wait_send()
    for side, step, device in peers():
        guarded(side, lambda a=(side, step, device): send_f(*a).wait_send())


def store(atm, ocean, atm_out, ocean_out, sem):
    copies = [pltpu.make_async_copy(ocean, ocean_out, sem.at[4])]
    copies += [pltpu.make_async_copy(atm.at[c, m], atm_out.at[c, m], sem.at[2 * c + m]) for c in range(2) for m in range(2)]
    for copy in copies:
        copy.start()
    for copy in copies:
        copy.wait()


def body(nx, nlat, atmosphere, ocean_state, viscosity, sea_mask, parameter_index, parameter_table, level_mix):
    lon = atmosphere.shape[4]
    quarter = lon // nx
    vmem = pl.BlockSpec(memory_space=pltpu.VMEM)
    hbm = pl.BlockSpec(memory_space=pltpu.HBM)
    anywhere = pl.BlockSpec(memory_space=pl.ANY)
    window = quarter // LANES
    members = 2 * nx
    dma = pltpu.SemaphoreType.DMA
    fields = jnp.transpose(atmosphere, (0, 1, 3, 2, 4))
    atm_out, ocean_out = pl.pallas_call(
        functools.partial(kernel, nx, nlat, 1.0 / (4 * nx)),
        out_shape=(
            jax.ShapeDtypeStruct(fields.shape, F32),
            jax.ShapeDtypeStruct((6, 2, 192), F32),
        ),
        in_specs=[hbm] * 7,
        out_specs=(vmem, vmem),
        scratch_shapes=[
            pltpu.VMEM((6, 2, 192), F32),
            pltpu.VMEM((6, 192), F32),
            pltpu.VMEM((6, lon), jnp.int32),
            pltpu.SMEM((2,), jnp.int32),
            pltpu.SMEM(parameter_table.shape[::-1], F32),
            pltpu.VMEM((8, 8), F32),
            pltpu.VMEM((6, 14, 2, 2, 8, lon), F32),
            pltpu.VMEM((2, 2, 2, 8, 8, LANES), F32),
            pltpu.VMEM((2, 2, 8, LANES), F32),
            pltpu.VMEM((2, 2, 8, LANES), F32),
            pltpu.VMEM((8, 2, 2, 8, lon), F32),
            pltpu.VMEM((2, 2, 16, lon), F32),
            pltpu.VMEM((2, 3, nx, 3, 8, 2 * LANES), F32),
            pltpu.VMEM((3, 8, lon), F32),
            pltpu.VMEM((2, 16, lon), F32),
            pltpu.VMEM((16, lon), F32),
            pltpu.VMEM((16, lon), F32),
            pltpu.VMEM((2, 16, lon), F32),
            pltpu.VMEM((2, lon // LANES + 2, 2, 8, LANES), F32),
            pltpu.VMEM((2, members - 1, window, 2, 8, LANES), F32),
            pltpu.VMEM((3, nx, window, 2, 8, LANES), F32),
            pltpu.VMEM((3, 8, 2 * LANES), F32),
            pltpu.VMEM((6, 2, 192), F32),
            pltpu.VMEM((6, 192), F32),
            pltpu.VMEM((2, 2, 8, LANES), F32),
            pltpu.VMEM((2, 8, lon), F32),
            dma((6,)),
            dma((2, 2, 4)),
            dma((2, 2, 4)),
            dma((2, 3, nx)),
            dma((2, 3, nx)),
            dma((2,)),
            dma((2,)),
            dma((2,)),
            dma((2,)),
            dma((2, members - 1)),
            dma((2, members - 1)),
            dma((3, nx)),
            dma((3, nx)),
            dma((6,)),
        ],
        compiler_params=pltpu.CompilerParams(
            collective_id=0, has_side_effects=True, vmem_limit_bytes=44 * 1024 * 1024
        ),
        name="coupled_window",
    )(
        *[
            pltpu.with_memory_space_constraint(operand, pltpu.HBM)
            for operand in (
                fields,
                jnp.transpose(ocean_state, (1, 0, 2)),
                viscosity,
                sea_mask,
                parameter_index,
                jnp.transpose(parameter_table),
                level_mix,
            )
        ]
    )
    atm_out, ocean_out = pl.pallas_call(
        store,
        out_shape=(jax.ShapeDtypeStruct(atm_out.shape, F32), jax.ShapeDtypeStruct(ocean_out.shape, F32)),
        in_specs=[anywhere] * 2,
        out_specs=(hbm, hbm),
        scratch_shapes=[dma((5,))],
        compiler_params=pltpu.CompilerParams(vmem_limit_bytes=1024 * 1024),
        name="store",
    )(atm_out, ocean_out)
    return jnp.transpose(atm_out, (0, 1, 3, 2, 4)), jnp.transpose(ocean_out, (1, 0, 2))


def solution(mesh):
    return jax.shard_map(
        functools.partial(body, mesh.shape["member"] // 2, mesh.shape["lat"]),
        mesh=mesh,
        in_specs=(
            P(None, "member", None, "lat", None),
            P(None, "lat", "member"),
            P("lat", "member"),
            P("lat", None),
            P("member"),
            P(),
            P(),
        ),
        out_specs=(P(None, "member", None, "lat", None), P(None, "lat", "member")),
        check_vma=False,
    )
```

```python
import functools

import jax
import jax.numpy as jnp
from jax import lax
from jax.experimental import pallas as pl
from jax.experimental.pallas import tpu as pltpu
from jax.sharding import PartitionSpec as P

ADVECTION = 0.1
OCEAN_GAIN = 0.5
OCEAN_DIFFUSION = 0.15
MESH = pl.DeviceIdType.MESH
F32 = jnp.float32
LANES = 128
CHUNK = 512


def tiles(vector, count):
    return jnp.concatenate([vector] * count, axis=1)


def sublane(shape):
    return lax.broadcasted_iota(jnp.int32, shape, 0)


def stack_rows(south, own, north):
    index = sublane(own.shape)
    middle = pltpu.roll(own, 5, 0)
    low = jnp.where(index < 5, pltpu.roll(south, 7, 0), middle)
    high = jnp.where(index < 3, middle, pltpu.roll(north, 3, 0))
    return jnp.concatenate([low, high], axis=0)


def join_chunks(even, odd):
    lane = lax.broadcasted_iota(jnp.int32, (8, LANES), 1)
    first = pltpu.roll(odd[:, :LANES], 64, 1)
    second = pltpu.roll(odd[:, LANES:], 64, 1)
    return jnp.concatenate(
        [even[:, :LANES], jnp.where(lane < 64, even[:, LANES:], first), jnp.where(lane < 64, first, second)], axis=1
    )


def kernel(
    nx, nlat, scale,
    atm, ocean_hbm, visc_hbm, mask_hbm, pick_hbm, table_hbm, mixing_hbm, atm_out, ocean_out,
    ocean_in, visc_in, mask_in, pick, table, mixing,
    state, coef, first, diff, surf, level, chunks, masks, ocean, visc, mask, force, part, gather_r, gather_f, seg,
    raw_ocean, raw_visc, bottom, tally,
    load_sem, halo_send, halo_recv, seg_send, seg_recv, pair_send, pair_recv, mask_send, mask_recv,
    r_send, r_recv, f_send, f_recv, small_sem,
):
    me = lax.axis_index("member")
    lat = lax.axis_index("lat")
    x, yh = lax.rem(me, nx), lax.div(me, nx)
    has_south, has_north = lat > 0, lat < nlat - 1
    partner = ((1 - yh) * nx + x, lat)
    lon = mask_in.shape[1]
    pieces = lon // CHUNK
    quarter = lon // nx
    columns = lon // LANES
    window = quarter // LANES
    members = 2 * nx

    def peers():
        for side in (-1, 1, 0):
            for step in (2, 1, 3, 0):
                if side or step:
                    yield side, step, (yh * nx + lax.rem(x + step, nx), lat + side)

    def guarded(side, run):
        if side < 0:
            pl.when(has_south)(run)
        elif side > 0:
            pl.when(has_north)(run)
        else:
            run()

    loads = [pltpu.make_async_copy(atm.at[:, :, r], state.at[0, r + 4], load_sem.at[r]) for r in range(6)]
    small = [
        pltpu.make_async_copy(source, target, small_sem.at[i])
        for i, (source, target) in enumerate(
            (
                (ocean_hbm, ocean_in), (visc_hbm, visc_in), (mask_hbm, mask_in),
                (pick_hbm, pick), (table_hbm, table), (mixing_hbm, mixing),
            )
        )
    ]
    for load in small:
        load.start()
    for load in loads:
        load.start()

    barrier = pltpu.get_barrier_semaphore()
    for step in range(1, members):
        device = (lax.rem(me + step, members), lat)
        pl.semaphore_signal(barrier, inc=1, device_id=device, device_id_type=MESH)
    for side, step, device in peers():
        if side:
            guarded(side, lambda device=device: pl.semaphore_signal(barrier, inc=1, device_id=device, device_id_type=MESH))

    pl.semaphore_wait(barrier, members - 1 + nx * has_south.astype(jnp.int32) + nx * has_north.astype(jnp.int32))

    def halo(cp, side, depth):
        row = 5 - depth if side > 0 else depth
        there = 3 - depth if side > 0 else 10 + depth
        source = atm.at[:, :, row] if cp == 0 else state.at[3, row + 4]
        k = (side + 1) // 2
        return pltpu.make_async_remote_copy(
            source, state.at[3 * cp, there], halo_send.at[cp, k, depth], halo_recv.at[cp, k, depth],
            device_id=(me, lat + side), device_id_type=MESH,
        )

    def start_halos(cp, depths):
        for depth in depths:
            for side in (-1, 1):
                guarded(side, lambda side=side, depth=depth: halo(cp, side, depth).start())

    def wait_halo(cp, depth):
        for side in (-1, 1):
            guarded(-side, lambda side=side: halo(cp, side, depth).wait_recv())

    def spread(stage, side, step, device):
        source = seg if stage == 0 else chunks.at[1 - yh, 1, x]
        target = chunks.at[yh if stage == 0 else 1 - yh, 1 - side, x]
        return pltpu.make_async_remote_copy(
            source, target, seg_send.at[stage, side + 1, step], seg_recv.at[stage, side + 1, step],
            device_id=device, device_id_type=MESH,
        )

    pairs = [
        pltpu.make_async_remote_copy(
            source, target, pair_send.at[k], pair_recv.at[k], device_id=partner, device_id_type=MESH
        )
        for k, (source, target) in enumerate(((ocean_hbm, raw_ocean), (visc_hbm, raw_visc)))
    ]

    def pack(ocean_ref, visc_ref):
        fields = []
        for field in range(3):
            lines = [visc_ref[r : r + 1, :] if field == 2 else ocean_ref[r, field : field + 1, :] for r in range(6)]
            block = jnp.concatenate(lines + [jnp.zeros((2, 192), F32)], axis=0)
            fields.append(jnp.concatenate([block, jnp.zeros((8, 64), F32)], axis=1))
        return jnp.stack(fields)

    def send_mask(side):
        return pltpu.make_async_remote_copy(
            masks.at[1], masks.at[1 - side], mask_send.at[(side + 1) // 2], mask_recv.at[(side + 1) // 2],
            device_id=(me, lat + side), device_id_type=MESH,
        )

    for pair in pairs:
        pair.start()
    start_halos(0, (0, 1, 2))
    for load in small:
        load.wait()

    own = pack(ocean_in, visc_in)
    seg[...] = own
    chunks[yh, 1, x] = own
    for side, step, device in peers():
        guarded(side, lambda a=(side, step, device): spread(0, *a).start())
    masks[1] = jnp.zeros((8, lon), F32)
    masks[1, 0:6, :] = mask_in[...].astype(F32)
    row_zero = jnp.zeros((2, 2, 8, lon), F32)

    @pl.when(lat == 0)
    def _():
        for b in range(6):
            state[b, 3] = row_zero
        masks[0] = jnp.zeros((8, lon), F32)
        for i in range(nx):
            gather_f[0, i] = jnp.zeros((window, 2, 8, LANES), F32)
            for a in range(2):
                chunks[a, 0, i] = jnp.zeros((3, 8, 2 * LANES), F32)

    @pl.when(lat == nlat - 1)
    def _():
        for b in range(6):
            state[b, 10] = row_zero
        masks[2] = jnp.zeros((8, lon), F32)
        for i in range(nx):
            gather_f[2, i] = jnp.zeros((window, 2, 8, LANES), F32)
            for a in range(2):
                chunks[a, 2, i] = jnp.zeros((3, 8, 2 * LANES), F32)


    sub = sublane((8, LANES))
    top = sub == 0
    dif = [0.6 * table[0, pick[m]] for m in range(2)]
    exc = [[2.0 * table[1 + c, pick[m]] for m in range(2)] for c in range(2)]
    exv = [[jnp.where(top, exc[c][m], 0.0) for m in range(2)] for c in range(2)]
    mix = mixing[...]
    row8 = lax.broadcasted_iota(jnp.int32, (8, 8), 0)
    col8 = lax.broadcasted_iota(jnp.int32, (8, 8), 1)
    for m in range(2):
        diff[m, 0] = jnp.full((8, LANES), dif[m], F32)
        diff[m, 1] = jnp.full((8, LANES), 1.0 - 4.0 * dif[m], F32) / diff[m, 0]
        diff[m, 0] = (0.5 * ADVECTION) / diff[m, 0]
    level_zero = [[jnp.zeros((8, LANES), F32) for m in range(2)] for c in range(2)]
    for r in range(8):
        diagonal = jnp.sum(jnp.where(col8 == lax.rem(row8 - r + 8, 8), mix, 0.0), axis=1, keepdims=True)
        value = jnp.broadcast_to(diagonal, (8, LANES))
        if r == 0:
            value = value + 1.0
        for c in range(2):
            for m in range(2):
                weight = dif[m] * jnp.where(top, value * (1.0 - exc[c][m]), value)
                others = jnp.where(sub == r, 0.0, weight)
                level_zero[c][m] = level_zero[c][m] + (weight - others)
                coef[0, c, m, r] = pltpu.roll(weight, 4, 0) if r >= 4 else weight
                coef[1, c, m, r] = pltpu.roll(others, 4, 0) if r >= 4 else others
    upper = jnp.sum(jnp.where(row8 == col8, jnp.broadcast_to(mix[0:1, :], (8, 8)), 0.0), axis=1, keepdims=True)
    upper = jnp.broadcast_to(upper, (8, LANES)) + jnp.where(top, 1.0, 0.0)
    share = [[exc[c][m] * (1.0 - exc[c][m]) for m in range(2)] for c in range(2)]
    for c in range(2):
        for m in range(2):
            first[c, m] = level_zero[c][m]
            bottom[c, m] = (share[c][m] * dif[m]) * upper

    def stencil(source, e, m, k):
        width = CHUNK // LANES
        off, right, left = k * CHUNK, (k + 1) % pieces * CHUNK, (k * CHUNK - LANES) % lon
        gain = tiles(diff[m, 0], width)
        keep = tiles(diff[m, 1], width)
        wind = None
        for c in (1, 0):
            centre = state[source, e, c, m, :, off : off + CHUNK]
            ahead = state[source, e, c, m, :, right : right + LANES]
            behind = state[source, e, c, m, :, left : left + LANES]
            north = state[source, e + 1, c, m, :, off : off + CHUNK]
            south = state[source, e - 1, c, m, :, off : off + CHUNK]
            east = pltpu.roll(jnp.concatenate([centre, ahead], axis=1), CHUNK + LANES - 1, 1)[:, :CHUNK]
            west = pltpu.roll(jnp.concatenate([centre, behind], axis=1), 1, 1)[:, :CHUNK]
            if c == 1:
                wind = gain * centre
            yield c, keep * centre + ((east + west) + (north + south)) - wind * (east - west)

    def mixed(advected, kind, c, m):
        width = CHUNK // LANES
        near = tiles(coef[kind, c, m, 0], width) * advected
        far = tiles(coef[kind, c, m, 4], width) * advected
        for r in range(1, 4):
            turned = pltpu.roll(advected, r, 0)
            near = near + tiles(coef[kind, c, m, r], width) * turned
            far = far + tiles(coef[kind, c, m, r + 4], width) * turned
        return near + pltpu.roll(far, 4, 0)

    def each_row(start, stride, count, run):
        def body(i, carry):
            row = start + i * stride
            inside = ((row >= 0) | has_south) & ((row <= 5) | has_north)
            pl.when(inside)(lambda: run(row))
            return carry

        lax.fori_loop(0, count, body, 0)

    def rows(source, target, start, stride, count, kind):
        def run(row):
            for m in range(2):
                for k in range(pieces):
                    for c, advected in stencil(source, row + 4, m, k):
                        state[target, row + 4, c, m, :, k * CHUNK : (k + 1) * CHUNK] = mixed(advected, kind, c, m)

        each_row(start, stride, count, run)

    def last_rows(source, target, start, count, shift):
        index = sublane((8, CHUNK))

        def run(row):
            for k in range(pieces):
                span = slice(k * CHUNK, (k + 1) * CHUNK)
                sums = [None, None]
                for m in range(2):
                    for c, advected in stencil(source, row + 4, m, k):
                        state[target, row + 4, c, m, :, span] = advected
                        term = tiles(bottom[c, m], CHUNK // LANES) * advected
                        sums[c] = term if sums[c] is None else sums[c] + term
                for c in range(2):
                    for turn in (4, 2, 1):
                        sums[c] = sums[c] + pltpu.roll(sums[c], turn, 0)
                    tally[c, :, span] = jnp.where(index == row + shift, sums[c], tally[c, :, span])

        for c in range(2):
            tally[c] = jnp.zeros((8, lon), F32)
        each_row(start, 1, count, run)

    def mix_rows(source, start, stride, count):
        def run(row):
            for m in range(2):
                for k in range(pieces):
                    span = slice(k * CHUNK, (k + 1) * CHUNK)
                    for c in range(2):
                        value = mixed(state[source, row + 4, c, m, :, span], 0, c, m) + surf[row + 1, c, m, :, span]
                        if source == 3:
                            state[3, row + 4, c, m, :, span] = value
                        else:
                            atm_out[c, m, row, :, span] = value

        each_row(start, stride, count, run)

    def before_surface(cp, deep, between):
        b = 3 * cp
        for depth in range(deep):
            if depth == (0 if cp else 2):
                between()
            wait_halo(cp, depth)
            rows(b, b + 1, -depth, 5 + 2 * depth, 2, 0)
            if depth == 0:
                rows(b + 1, b + 2, 1, 1, 4, 1)
            else:
                rows(b + 1, b + 2, 1 - depth, 3 + 2 * depth, 2, 1)
        for row in range(1 - deep, 5 + deep):
            for c in range(2):
                for m in range(2):
                    level[c, m, row + 5 : row + 6, :] = state[b + 1, row + 4, c, m, 0:1, :]

    def add_surface(cp, deep):
        b = 3 * cp
        for m in range(2):
            keep, gain = tiles(diff[m, 1], columns), tiles(diff[m, 0], columns)
            keep, gain = jnp.concatenate([keep] * 2, axis=0), jnp.concatenate([gain] * 2, axis=0)
            wind = None
            for c in (1, 0):
                here = level[c, m] + exc[c][m] * ocean[c]
                if c == 1:
                    wind = gain * here
                east, west = pltpu.roll(here, lon - 1, 1), pltpu.roll(here, 1, 1)
                around = (east + west) + (pltpu.roll(here, 15, 0) + pltpu.roll(here, 1, 0))
                level[c, m] = keep * here + around - wind * (east - west)
        for row in range(2 - deep, 4 + deep):
            for c in range(2):
                line = jnp.broadcast_to(ocean[c, row + 5 : row + 6, :], (8, lon))
                for m in range(2):
                    value = tiles(exv[c][m], columns) * line
                    if 3 - deep <= row < 3 + deep:
                        surf[row + 1, c, m] = value

                    def run(value=value, c=c, m=m, row=row):
                        lowest = jnp.broadcast_to(level[c, m, row + 5 : row + 6, :], (8, lon))
                        change = tiles(first[c, m], columns) * lowest + value
                        state[b + 2, row + 4, c, m] = state[b + 2, row + 4, c, m] + change

                    guarded(-1 if row < 0 else 1 if row > 5 else 0, run)

    def advance(here, rate, sea, drive):
        width = here.shape[1]
        lap = (
            pltpu.roll(here, width - 1, 1) + pltpu.roll(here, 1, 1)
            + pltpu.roll(here, 15, 0) + pltpu.roll(here, 1, 0) - 4.0 * here
        )
        return here + sea * (OCEAN_GAIN * drive + rate * lap)

    def ocean_steps():
        for c in range(2):
            for q in range(nx):
                for j in range(window):
                    blocks = [gather_f[side, q, j, c] for side in range(3)]
                    start = q * quarter + j * LANES
                    force[c, :, start : start + LANES] = stack_rows(*blocks)
        for _ in range(2):
            for c in range(2):
                rate = visc[...] if c == 1 else OCEAN_DIFFUSION
                ocean[c] = advance(ocean[c], rate, mask[...], force[c])

    def first_tile(cp, member):
        if cp == 0:
            return window * lax.rem(member, nx)
        return lax.rem(lax.div(3 * member + 2 * columns - 1, 2), columns)

    def send_r(cp, step):
        to = lax.rem(me + step, members)
        return pltpu.make_async_remote_copy(
            part.at[cp, pl.ds(first_tile(cp, to), window)], gather_r.at[cp, step - 1],
            r_send.at[cp, step - 1], r_recv.at[cp, step - 1], device_id=(to, lat), device_id_type=MESH,
        )

    def send_f(side, step, device):
        return pltpu.make_async_remote_copy(
            gather_f.at[1, x], gather_f.at[1 - side, x], f_send.at[side + 1, step],
            f_recv.at[side + 1, step], device_id=device, device_id_type=MESH,
        )

    def flux(cp):
        for c in range(2):
            own = pltpu.roll(ocean[c], 11 + cp, 0)[0:8]
            value = tally[c] - (share[c][0] + share[c][1]) * own
            for j in range(columns + 2):
                start = j % columns * LANES
                part[cp, j, c] = value[:, start : start + LANES]
        for step in (2, 6, 3, 5, 4, 1, 7):
            send_r(cp, step).start()

    def total(cp):
        for step in range(1, members):
            send_r(cp, step).wait_recv()
        parts = [part[cp, pl.ds(first_tile(cp, me), window)]] + [gather_r[cp, k] for k in range(members - 1)]
        while len(parts) > 1:
            parts = [a + b for a, b in zip(parts[0::2], parts[1::2])]
        return parts[0] * scale

    for load in loads:
        load.wait()
    rows(0, 1, 1, 1, 4, 0)
    for pair in pairs:
        pair.wait_recv()
    chunks[1 - yh, 1, x] = pack(raw_ocean, raw_visc)
    for side, step, device in peers():
        guarded(side, lambda a=(side, step, device): spread(1, *a).start())
    for side in (-1, 1):
        guarded(side, lambda side=side: send_mask(side).start())

    def assemble():
        for stage in range(2):
            for side, step, device in peers():
                guarded(-side, lambda a=(stage, side, step, device): spread(*a).wait_recv())
        for field in range(3):
            for q in range(nx):
                blocks = []
                for side in range(3):
                    even = chunks[(2 * q) // nx, side, (2 * q) % nx, field]
                    odd = chunks[(2 * q + 1) // nx, side, (2 * q + 1) % nx, field]
                    blocks.append(join_chunks(even, odd))
                value = stack_rows(*blocks)
                span = slice(q * quarter, (q + 1) * quarter)
                if field == 2:
                    visc[:, span] = value
                else:
                    ocean[field, :, span] = value

    before_surface(0, 3, assemble)
    add_surface(0, 3)
    last_rows(2, 3, 0, 6, 0)
    flux(0)
    mix_rows(3, 0, 5, 2)
    start_halos(1, (0,))
    mix_rows(3, 1, 3, 2)
    start_halos(1, (1,))
    mix_rows(3, 2, 1, 2)
    start_halos(1, (2, 3))
    rows(3, 4, 1, 1, 4, 0)

    def broadcast():
        gather_f[1, x] = total(0)
        for side, step, device in peers():
            guarded(side, lambda a=(side, step, device): send_f(*a).start())

    before_surface(1, 4, broadcast)
    for side in (-1, 1):
        guarded(-side, lambda side=side: send_mask(side).wait_recv())
    mask[...] = stack_rows(masks[0], masks[1], masks[2])
    for side, step, device in peers():
        guarded(-side, lambda a=(side, step, device): send_f(*a).wait_recv())
    ocean_steps()

    add_surface(1, 4)
    last_rows(5, 0, -1, 8, 1)
    flux(1)
    mix_rows(0, 0, 1, 6)
    starts = [pl.multiple_of(lax.rem(first_tile(1, me) + j, columns) * LANES, LANES) for j in range(window)]

    def windowed(ref, *lead):
        return jnp.concatenate([ref[(*lead, slice(None), pl.ds(start, LANES))] for start in starts], axis=1)

    here = [windowed(ocean, c) for c in range(2)]
    rates = [OCEAN_DIFFUSION, windowed(visc)]
    sea = windowed(mask)
    odd = lax.rem(me, 2) == 1
    final = total(1)
    for c in range(2):
        drive = jnp.concatenate([jnp.concatenate([pltpu.roll(final[j, c], 4, 0)] * 2, axis=0) for j in range(window)], axis=1)
        value = advance(advance(here[c], rates[c], sea, drive), rates[c], sea, drive)
        value = jnp.where(odd, pltpu.roll(value, 64, 1), value)
        for r in range(6):
            ocean_out[r, c : c + 1, :] = value[r + 5 : r + 6, LANES : LANES + 192]

    for pair in pairs:
        pair.wait_send()
    for side in (-1, 1):
        guarded(side, lambda side=side: send_mask(side).wait_send())
        for cp in range(2):
            for depth in range(3 + cp):
                guarded(side, lambda a=(cp, side, depth): halo(*a).wait_send())
    for stage in range(2):
        for side, step, device in peers():
            guarded(side, lambda a=(stage, side, step, device): spread(*a).wait_send())
    for cp in range(2):
        for step in range(1, members):
            send_r(cp, step).wait_send()
    for side, step, device in peers():
        guarded(side, lambda a=(side, step, device): send_f(*a).wait_send())


def store(atm, ocean, atm_out, ocean_out, sem):
    copies = [pltpu.make_async_copy(ocean, ocean_out, sem.at[4])]
    copies += [pltpu.make_async_copy(atm.at[c, m], atm_out.at[c, m], sem.at[2 * c + m]) for c in range(2) for m in range(2)]
    for copy in copies:
        copy.start()
    for copy in copies:
        copy.wait()


def body(nx, nlat, atmosphere, ocean_state, viscosity, sea_mask, parameter_index, parameter_table, level_mix):
    lon = atmosphere.shape[4]
    quarter = lon // nx
    vmem = pl.BlockSpec(memory_space=pltpu.VMEM)
    hbm = pl.BlockSpec(memory_space=pltpu.HBM)
    anywhere = pl.BlockSpec(memory_space=pl.ANY)
    window = quarter // LANES
    members = 2 * nx
    dma = pltpu.SemaphoreType.DMA
    fields = jnp.transpose(atmosphere, (0, 1, 3, 2, 4))
    atm_out, ocean_out = pl.pallas_call(
        functools.partial(kernel, nx, nlat, 1.0 / (4 * nx)),
        out_shape=(
            jax.ShapeDtypeStruct(fields.shape, F32),
            jax.ShapeDtypeStruct((6, 2, 192), F32),
        ),
        in_specs=[hbm] * 7,
        out_specs=(vmem, vmem),
        scratch_shapes=[
            pltpu.VMEM((6, 2, 192), F32),
            pltpu.VMEM((6, 192), F32),
            pltpu.VMEM((6, lon), jnp.int32),
            pltpu.SMEM((2,), jnp.int32),
            pltpu.SMEM(parameter_table.shape[::-1], F32),
            pltpu.VMEM((8, 8), F32),
            pltpu.VMEM((6, 14, 2, 2, 8, lon), F32),
            pltpu.VMEM((2, 2, 2, 8, 8, LANES), F32),
            pltpu.VMEM((2, 2, 8, LANES), F32),
            pltpu.VMEM((2, 2, 8, LANES), F32),
            pltpu.VMEM((8, 2, 2, 8, lon), F32),
            pltpu.VMEM((2, 2, 16, lon), F32),
            pltpu.VMEM((2, 3, nx, 3, 8, 2 * LANES), F32),
            pltpu.VMEM((3, 8, lon), F32),
            pltpu.VMEM((2, 16, lon), F32),
            pltpu.VMEM((16, lon), F32),
            pltpu.VMEM((16, lon), F32),
            pltpu.VMEM((2, 16, lon), F32),
            pltpu.VMEM((2, lon // LANES + 2, 2, 8, LANES), F32),
            pltpu.VMEM((2, members - 1, window, 2, 8, LANES), F32),
            pltpu.VMEM((3, nx, window, 2, 8, LANES), F32),
            pltpu.VMEM((3, 8, 2 * LANES), F32),
            pltpu.VMEM((6, 2, 192), F32),
            pltpu.VMEM((6, 192), F32),
            pltpu.VMEM((2, 2, 8, LANES), F32),
            pltpu.VMEM((2, 8, lon), F32),
            dma((6,)),
            dma((2, 2, 4)),
            dma((2, 2, 4)),
            dma((2, 3, nx)),
            dma((2, 3, nx)),
            dma((2,)),
            dma((2,)),
            dma((2,)),
            dma((2,)),
            dma((2, members - 1)),
            dma((2, members - 1)),
            dma((3, nx)),
            dma((3, nx)),
            dma((6,)),
        ],
        compiler_params=pltpu.CompilerParams(
            collective_id=0, has_side_effects=True, vmem_limit_bytes=44 * 1024 * 1024
        ),
        name="coupled_window",
    )(
        *[
            pltpu.with_memory_space_constraint(operand, pltpu.HBM)
            for operand in (
                fields,
                jnp.transpose(ocean_state, (1, 0, 2)),
                viscosity,
                sea_mask,
                parameter_index,
                jnp.transpose(parameter_table),
                level_mix,
            )
        ]
    )
    atm_out, ocean_out = pl.pallas_call(
        store,
        out_shape=(jax.ShapeDtypeStruct(atm_out.shape, F32), jax.ShapeDtypeStruct(ocean_out.shape, F32)),
        in_specs=[anywhere] * 2,
        out_specs=(hbm, hbm),
        scratch_shapes=[dma((5,))],
        compiler_params=pltpu.CompilerParams(vmem_limit_bytes=1024 * 1024),
        name="store",
    )(atm_out, ocean_out)
    return jnp.transpose(atm_out, (0, 1, 3, 2, 4)), jnp.transpose(ocean_out, (1, 0, 2))


def solution(mesh):
    return jax.shard_map(
        functools.partial(body, mesh.shape["member"] // 2, mesh.shape["lat"]),
        mesh=mesh,
        in_specs=(
            P(None, "member", None, "lat", None),
            P(None, "lat", "member"),
            P("lat", "member"),
            P("lat", None),
            P("member"),
            P(),
            P(),
        ),
        out_specs=(P(None, "member", None, "lat", None), P(None, "lat", "member")),
        check_vma=False,
    )
```
